512 devices in a mesh: ctx: 32 (over z_lo, x, core), tp: 16 (over z_hi, y).
Axes of the slice: x: 4, y: 8, z: 8 (z_hi: 2, z_lo: 4; z = z_hi * 4 + z_lo), core: 2. Of those that a mesh axis runs over, the one named last changes fastest.
Arguments:
- queries: bfloat16 [8192, 8192], P('ctx', 'tp'), may hold values from -100 to 100
- key_rows: bfloat16 [8192, 1024], P('ctx'), may hold values from -5 to 5
- value_rows: bfloat16 [8192, 1024], P('ctx'), may hold values from -6 to 6
- documents: int32 [8192], P('ctx'), may hold values from 0 to 3, never falling along the last dimension, each value on 1 to 6144 neighbouring positions
- out_weight: bfloat16 [8192, 8192], P('tp', 'ctx'), may hold values from -0.75 to 0.75
Outputs:
- attention_out: bfloat16 [8192, 8192], P(('ctx', 'tp'))
The draws below stay inside these ranges and needn't reach their ends.
Inputs may be any that keep to these rules, and one draw needn't show every extreme that they name: `documents`: document numbers never fall along the window; each document holds 1 to 6144 tokens and one holds exactly 6144.
All inputs are finite; a program needn't handle non-finite values.
Results may differ from the reference program's by a relative error of at most 0.015.
Values may be sent and summed in bfloat16 or wider, within the bound.
No kernel may reach another device: no remote copies, remote signals or barrier semaphores. Data moves between devices by JAX's collectives and lax.ppermute only.
A program may use at most 128 MiB of HBM per device.

```python
import math
import jax
import jax.numpy as jnp
import numpy as np
from jax import lax

D = 8192
HEADS = 64
KV_HEADS = 8
HD = 128
DOCS = 4
SEQ = 8192
MOST = 6144
N_TP = 16


def draw_together(key):
    key_base = jnp.clip(jax.random.normal(jax.random.fold_in(key, 101), (SEQ, KV_HEADS, HD), jnp.float32), -4.5, 4.5)
    query_base = jnp.clip(jax.random.normal(jax.random.fold_in(key, 102), (SEQ, HEADS, HD), jnp.float32), -5.0, 5.0)
    return (query_base.reshape(SEQ, HEADS * HD), key_base.reshape(SEQ, KV_HEADS * HD))


def draw_queries(key, part):
    return draw_together(key)[0].astype(jnp.bfloat16)


def draw_key_rows(key, part):
    return draw_together(key)[1].astype(jnp.bfloat16)


def steps_of(rng, extent, shards, least, largest):
    level = 1.0
    for axis_at, shards_of in shards:
        heights = jax.random.uniform(jax.random.fold_in(jax.random.fold_in(rng, 6), axis_at), (shards_of,), jnp.float32, least / len(shards), largest / len(shards))
        level = level * jnp.repeat(jnp.exp(heights), extent[axis_at] // shards_of).reshape((-1,) + (1,) * (len(extent) - 1 - axis_at))
    return level


def profile(count, total, most, skew):
    weights = [(1 << 20) // math.isqrt(grade ** skew) + 1 for grade in range(2, count + 1)]
    surplus, counts = total - most - (count - 1), [1] * (count - 1)
    while surplus > 0:
        movable = [i for i in range(count - 1) if counts[i] < most]
        pool, budget = sum([weights[i] for i in movable]), surplus
        for i in movable:
            addition = min(most - counts[i], max(1, budget * weights[i] // pool), surplus)
            counts[i] = counts[i] + addition
            surplus = surplus - addition
    return np.array([most] + counts)


def ragged_sizes(key, number_of, total, bound, lean):
    if number_of == 2:
        one = jax.random.randint(key, (), max(1, total - bound), min(bound, total - 1) + 1)
        return jnp.stack([one, total - one])
    tallies = jnp.asarray(profile(number_of, total, bound, lean), jnp.int32)
    pairs = (number_of - 1) // 2
    source_of, sink = tallies[1:1 + 2 * pairs:2], tallies[2:2 + 2 * pairs:2]
    room = jnp.minimum(source_of - 1, bound - sink)
    moved = jax.random.randint(jax.random.fold_in(key, 1), (pairs,), 0, 1 << 20) % (room + 1)
    tallies = tallies.at[1:1 + 2 * pairs:2].set(source_of - moved).at[2:2 + 2 * pairs:2].set(sink + moved)
    return tallies[jax.random.permutation(jax.random.fold_in(key, 2), number_of)]


def gaussian(rng, extent, deviation, reach, split=(), held_as=jnp.bfloat16):
    factor_of = steps_of(rng, extent, split, -0.22, 0.18) if split else 1.0
    values = jax.random.normal(rng, extent, jnp.float32) * deviation * factor_of
    return jnp.minimum(jnp.maximum(values, -reach), reach).astype(held_as)


def setup_inputs(seed: int = 0) -> dict:
    key_list = jax.random.split(jax.random.key(seed), 6)
    return {
        "queries": draw_queries(jax.random.fold_in(key_list[5], 71), 0),
        "key_rows": draw_key_rows(jax.random.fold_in(key_list[5], 71), 0),
        "value_rows": gaussian(key_list[2], (SEQ, KV_HEADS * HD), 1.0, 6.0, ((0, 32),)),
        "documents": jnp.searchsorted(jnp.cumsum(ragged_sizes(key_list[3], DOCS, SEQ, MOST, 0)), jnp.arange(SEQ), side="right").astype(jnp.int32),
        "out_weight": gaussian(key_list[4], (HEADS * HD, D), (HD // 2) ** -0.5, 0.75, ((0, 16), (1, 32))),
    }


def head_output(queries, key_rows, value_rows, documents, head_index):
    group_size = HEADS // KV_HEADS
    query_cols = lax.dynamic_slice_in_dim(queries, (head_index * HD).astype(jnp.int32), HD, 1)
    kv_start = (head_index // group_size * HD).astype(jnp.int32)
    key_cols = lax.dynamic_slice_in_dim(key_rows, kv_start, HD, 1)
    value_cols = lax.dynamic_slice_in_dim(value_rows, kv_start, HD, 1)
    scores = jnp.dot(query_cols, key_cols.T, preferred_element_type=jnp.float32) * (1.0 / math.sqrt(HD))
    position = jnp.arange(SEQ, dtype=jnp.int32)
    allowed = (position[None, :] <= position[:, None]) & (documents[None, :] == documents[:, None])
    row_max = lax.optimization_barrier(jnp.max(jnp.where(allowed, scores, -1e+30), axis=1, keepdims=True))
    weights = jnp.where(allowed, jnp.exp(scores - row_max), 0.0)
    denominator = lax.optimization_barrier(jnp.sum(weights, axis=1, keepdims=True))
    weighted = jnp.dot(weights.astype(jnp.bfloat16), value_cols, preferred_element_type=jnp.float32)
    return (weighted / denominator).astype(jnp.bfloat16)

def reference(queries, key_rows, value_rows, documents, out_weight):
    heads_out = lax.map(lambda head_index: head_output(queries, key_rows, value_rows, documents, head_index), jnp.arange(HEADS, dtype=jnp.int32))
    attended = jnp.transpose(heads_out, (1, 0, 2)).reshape(SEQ, HEADS * HD)
    block_width = HEADS * HD // N_TP

    def accumulate(group_index, running):
        begin = (group_index * block_width).astype(jnp.int32)
        columns = lax.dynamic_slice_in_dim(attended, begin, block_width, 1)
        weight_rows = lax.dynamic_slice_in_dim(out_weight, begin, block_width, 0)
        partial_sum = jnp.dot(columns, weight_rows, preferred_element_type=jnp.float32)
        rounded = lax.optimization_barrier(partial_sum.astype(jnp.bfloat16))
        return running + rounded.astype(jnp.float32)
    summed = lax.fori_loop(0, N_TP, accumulate, jnp.zeros((SEQ, D), jnp.float32))
    return summed.astype(jnp.bfloat16)
```

```python
import functools
import math

import jax
import jax.numpy as jnp
from jax import lax
from jax.experimental import pallas as pl
from jax.experimental.pallas import tpu as pltpu
from jax.sharding import Mesh, PartitionSpec as P

HEADS = 64
KV_HEADS = 8
HD = 128
ZL, X, CORE, ZH, Y = 4, 4, 2, 2, 8
AXES = ("zl", "x", "core", "zh", "y")
CTX = ("zl", "x", "core")
TP = ("zh", "y")
PAD = 8
NEG = -1e30
SCALE2 = math.log2(math.e) / math.sqrt(HD)


def attend_kernel(heads, sources, first, last, where_ref, q_ref, docs_ref, *refs):
    n = len(sources)
    pieces = refs[: 2 * n]
    refs = refs[2 * n :]
    if not first:
        m_in, acc_in = refs[:2]
        refs = refs[2:]
    if last:
        out_ref, m_ref, acc_ref = refs
    else:
        m_ref, acc_ref = refs
    rows = q_ref.shape[0]
    my_z, my_x, my_core = where_ref[0], where_ref[1], where_ref[2]
    my_block = my_z * X + my_x
    if first:
        m_ref[...] = jnp.full_like(m_ref, NEG)
        acc_ref[...] = jnp.zeros_like(acc_ref)
    else:
        m_ref[...] = m_in[...]
        acc_ref[...] = acc_in[...]
    q_docs = docs_ref[...]
    q_first, q_last = jnp.min(q_docs), jnp.max(q_docs)
    ones = jnp.ones((rows, HD), jnp.bfloat16)

    for at, (offset, z_from, z_count) in enumerate(sources):
        own, other = pieces[2 * at], pieces[2 * at + 1]
        their_x = lax.rem(my_x + offset, X)

        def block(z, carry, own=own, other=other, their_x=their_x, z_from=z_from):
            their_block = (z_from + z) * X + their_x
            docs_own = own[z, rows : rows + PAD, :].astype(jnp.float32)
            docs_other = other[z, rows : rows + PAD, :].astype(jnp.float32)
            k_first = jnp.min(jnp.minimum(docs_own, docs_other))
            k_last = jnp.max(jnp.maximum(docs_own, docs_other))
            needed = (their_block <= my_block) & (k_last >= q_first)
            whole = needed & (their_block < my_block) & (k_first >= q_last)

            def update(masked):
                if masked:
                    row = lax.broadcasted_iota(jnp.int32, (rows, rows), 0)
                    lane = lax.broadcasted_iota(jnp.int32, (rows, rows), 1)
                    q_pos = my_block * (2 * rows) + my_core * rows + row
                    k_pos = their_block * (2 * rows) + lane
                    allowed = []
                    for side, docs in ((my_core, docs_own), (1 - my_core, docs_other)):
                        same = jnp.broadcast_to(docs[:1], (rows, rows)) == jnp.concatenate(
                            [q_docs] * (rows // HD), axis=1
                        )
                        allowed.append(same & (k_pos + side * rows <= q_pos))
                values = [
                    jnp.concatenate([ref[z, :rows, HD:], ones], axis=1) for ref in (own, other)
                ]
                for h in range(heads):
                    q = q_ref[:, h * HD : (h + 1) * HD]
                    scores = [
                        lax.dot_general(
                            q,
                            ref[z, :rows, :HD],
                            (((1,), (1,)), ((), ())),
                            preferred_element_type=jnp.float32,
                        )
                        for ref in (own, other)
                    ]
                    if masked:
                        scores = [jnp.where(a, s, NEG) for a, s in zip(allowed, scores)]
                    old = m_ref[h]
                    top = jnp.max(jnp.maximum(scores[0], scores[1]), axis=1, keepdims=True)
                    new = jnp.maximum(old, top)
                    wide = jnp.concatenate([new] * (rows // HD), axis=1)
                    total = None
                    for side in range(2):
                        weights = jnp.exp2((scores[side] - wide) * SCALE2)
                        if masked:
                            weights = jnp.where(allowed[side], weights, 0.0)
                        term = jnp.dot(
                            weights.astype(jnp.bfloat16),
                            values[side],
                            preferred_element_type=jnp.float32,
                        )
                        total = term if total is None else total + term
                    keep = jnp.exp2((old - new) * SCALE2)
                    m_ref[h] = new
                    acc_ref[h] = acc_ref[h] * jnp.concatenate([keep, keep], axis=1) + total

            @pl.when(whole)
            def _():
                update(False)

            @pl.when(needed & jnp.logical_not(whole))
            def _():
                update(True)

            return carry

        lax.fori_loop(0, z_count, block, 0)

    if last:
        part = rows // (ZH * Y)
        for h in range(heads):
            done = (acc_ref[h, :, :HD] / acc_ref[h, :, HD:]).astype(jnp.bfloat16)
            for zh in range(ZH):
                for y in range(Y):
                    source = (zh * Y + y) * part
                    target = (y * ZH + zh) * part
                    out_ref[target : target + part, h * HD : (h + 1) * HD] = done[
                        source : source + part
                    ]


def attend(where, q, docs, pieces, sources, state, last):
    rows, width = q.shape
    heads = width // HD
    first = state is None
    states = (
        jax.ShapeDtypeStruct((heads, rows, HD), jnp.float32),
        jax.ShapeDtypeStruct((heads, rows, 2 * HD), jnp.float32),
    )
    vmem = pl.BlockSpec(memory_space=pltpu.VMEM)
    inputs = [q, docs, *pieces] + ([] if first else list(state))
    blocks = sum(s[2] for s in sources)
    return pl.pallas_call(
        functools.partial(attend_kernel, heads, sources, first, last),
        out_shape=jax.ShapeDtypeStruct((rows, width), jnp.bfloat16) if last else states,
        in_specs=[pl.BlockSpec(memory_space=pltpu.SMEM)] + [vmem] * len(inputs),
        out_specs=vmem if last else (vmem, vmem),
        scratch_shapes=[pltpu.VMEM(s.shape, s.dtype) for s in states] if last else [],
        compiler_params=pltpu.CompilerParams(vmem_limit_bytes=40 << 20),
        cost_estimate=pl.CostEstimate(
            flops=blocks * heads * rows * 2 * rows * HD * 6,
            bytes_accessed=blocks * rows * HD * 8,
            transcendentals=blocks * heads * rows * 2 * rows,
        ),
    )(where, *inputs)


def around(value, axis, size, step):
    return lax.ppermute(value, axis, [(i, (i + step) % size) for i in range(size)])


def on_device(queries, key_rows, value_rows, documents, out_weight):
    rows = queries.shape[0]
    heads_here = queries.shape[1] // HD
    kv = lax.axis_index(TP) * heads_here // (HEADS // KV_HEADS)
    own_keys = lax.dynamic_slice_in_dim(key_rows, kv * HD, HD, 1)
    own_values = lax.dynamic_slice_in_dim(value_rows, kv * HD, HD, 1)
    weight = lax.all_gather(out_weight, CTX, axis=1, tiled=True)
    doc_rows = jnp.broadcast_to(documents.astype(jnp.bfloat16)[None, :], (PAD, rows))
    packed = jnp.concatenate(
        [jnp.concatenate([own_keys, own_values], axis=1), doc_rows], axis=0
    )
    where = jnp.stack([lax.axis_index(a) for a in CTX]).astype(jnp.int32)
    docs = jnp.broadcast_to(documents.astype(jnp.float32)[:, None], (rows, HD))

    mine = lax.all_gather(packed, "zl", axis=0)
    left = around(mine, "x", X, 1)
    right = around(mine, "x", X, -1)
    mine_other = around(mine, "core", CORE, 1)
    far_a = around(left[: ZL // 2], "x", X, 1)
    far_b = around(right[ZL // 2 :], "x", X, -1)
    left_other = around(left, "core", CORE, 1)
    right_other = around(right, "core", CORE, 1)
    far_a_other = around(far_a, "core", CORE, 1)
    far_b_other = around(far_b, "core", CORE, 1)

    state = attend(where, queries, docs, [mine, mine_other], [(0, 0, ZL)], None, False)
    state = attend(
        where,
        queries,
        docs,
        [left, left_other, right, right_other],
        [(X - 1, 0, ZL), (1, 0, ZL)],
        state,
        False,
    )
    attended = attend(
        where,
        queries,
        docs,
        [far_a, far_a_other, far_b, far_b_other],
        [(2, 0, ZL // 2), (2, ZL // 2, ZL // 2)],
        state,
        True,
    )
    terms = jnp.dot(attended, weight, preferred_element_type=jnp.float32).astype(jnp.bfloat16)
    over_y = lax.psum_scatter(terms, "y", scatter_dimension=0, tiled=True)
    part = over_y.shape[0] // ZH
    zh = lax.axis_index("zh")
    keep = lax.dynamic_slice_in_dim(over_y, zh * part, part, 0)
    give = lax.dynamic_slice_in_dim(over_y, (1 - zh) * part, part, 0)
    came = around(give, "zh", ZH, 1)
    return (keep.astype(jnp.float32) + came.astype(jnp.float32)).astype(jnp.bfloat16)


def solution(mesh):
    fine = Mesh(mesh.devices.reshape(ZL, X, CORE, ZH, Y), AXES)
    in_specs = (P(CTX, TP), P(CTX, None), P(CTX, None), P(CTX), P(TP, CTX))
    return jax.shard_map(
        on_device, mesh=fine, in_specs=in_specs, out_specs=P(CTX + TP, None), check_vma=False
    )
```

```python
import functools
import math

import jax
import jax.numpy as jnp
from jax import lax
from jax.experimental import pallas as pl
from jax.experimental.pallas import tpu as pltpu
from jax.sharding import Mesh, PartitionSpec as P

HEADS = 64
KV_HEADS = 8
HD = 128
ZL, X, CORE, ZH, Y = 4, 4, 2, 2, 8
AXES = ("zl", "x", "core", "zh", "y")
CTX = ("zl", "x", "core")
TP = ("zh", "y")
PAD = 8
NEG = -1e30
SCALE2 = math.log2(math.e) / math.sqrt(HD)


def attend_kernel(heads, sources, first, last, where_ref, q_ref, docs_ref, *refs):
    n = len(sources)
    pieces = refs[: 2 * n]
    refs = refs[2 * n :]
    if not first:
        m_in, acc_in = refs[:2]
        refs = refs[2:]
    if last:
        out_ref, m_ref, acc_ref = refs
    else:
        m_ref, acc_ref = refs
    rows = q_ref.shape[0]
    my_z, my_x, my_core = where_ref[0], where_ref[1], where_ref[2]
    my_block = my_z * X + my_x
    if first:
        m_ref[...] = jnp.full_like(m_ref, NEG)
        acc_ref[...] = jnp.zeros_like(acc_ref)
    else:
        m_ref[...] = m_in[...]
        acc_ref[...] = acc_in[...]
    q_docs = docs_ref[...]
    q_first, q_last = jnp.min(q_docs), jnp.max(q_docs)
    ones = jnp.ones((rows, HD), jnp.bfloat16)

    for at, (offset, z_from, z_count) in enumerate(sources):
        own, other = pieces[2 * at], pieces[2 * at + 1]
        their_x = lax.rem(my_x + offset, X)

        def block(z, carry, own=own, other=other, their_x=their_x, z_from=z_from):
            their_block = (z_from + z) * X + their_x
            docs_own = own[z, rows : rows + PAD, :].astype(jnp.float32)
            docs_other = other[z, rows : rows + PAD, :].astype(jnp.float32)
            k_first = jnp.min(jnp.minimum(docs_own, docs_other))
            k_last = jnp.max(jnp.maximum(docs_own, docs_other))
            needed = (their_block <= my_block) & (k_last >= q_first)
            whole = needed & (their_block < my_block) & (k_first >= q_last)

            def update(masked):
                if masked:
                    row = lax.broadcasted_iota(jnp.int32, (rows, rows), 0)
                    lane = lax.broadcasted_iota(jnp.int32, (rows, rows), 1)
                    q_pos = my_block * (2 * rows) + my_core * rows + row
                    k_pos = their_block * (2 * rows) + lane
                    allowed = []
                    for side, docs in ((my_core, docs_own), (1 - my_core, docs_other)):
                        same = jnp.broadcast_to(docs[:1], (rows, rows)) == jnp.concatenate(
                            [q_docs] * (rows // HD), axis=1
                        )
                        allowed.append(same & (k_pos + side * rows <= q_pos))
                values = [
                    jnp.concatenate([ref[z, :rows, HD:], ones], axis=1) for ref in (own, other)
                ]
                for h in range(heads):
                    q = q_ref[:, h * HD : (h + 1) * HD]
                    scores = [
                        lax.dot_general(
                            q,
                            ref[z, :rows, :HD],
                            (((1,), (1,)), ((), ())),
                            preferred_element_type=jnp.float32,
                        )
                        for ref in (own, other)
                    ]
                    if masked:
                        scores = [jnp.where(a, s, NEG) for a, s in zip(allowed, scores)]
                    old = m_ref[h]
                    top = jnp.max(jnp.maximum(scores[0], scores[1]), axis=1, keepdims=True)
                    new = jnp.maximum(old, top)
                    wide = jnp.concatenate([new] * (rows // HD), axis=1)
                    total = None
                    for side in range(2):
                        weights = jnp.exp2((scores[side] - wide) * SCALE2)
                        if masked:
                            weights = jnp.where(allowed[side], weights, 0.0)
                        term = jnp.dot(
                            weights.astype(jnp.bfloat16),
                            values[side],
                            preferred_element_type=jnp.float32,
                        )
                        total = term if total is None else total + term
                    keep = jnp.exp2((old - new) * SCALE2)
                    m_ref[h] = new
                    acc_ref[h] = acc_ref[h] * jnp.concatenate([keep, keep], axis=1) + total

            @pl.when(whole)
            def _():
                update(False)

            @pl.when(needed & jnp.logical_not(whole))
            def _():
                update(True)

            return carry

        lax.fori_loop(0, z_count, block, 0)

    if last:
        for h in range(heads):
            done = (acc_ref[h, :, :HD] / acc_ref[h, :, HD:]).astype(jnp.bfloat16)
            out_ref[:, h * HD : (h + 1) * HD] = done


def attend(where, q, docs, pieces, sources, state, last):
    rows, width = q.shape
    heads = width // HD
    first = state is None
    states = (
        jax.ShapeDtypeStruct((heads, rows, HD), jnp.float32),
        jax.ShapeDtypeStruct((heads, rows, 2 * HD), jnp.float32),
    )
    vmem = pl.BlockSpec(memory_space=pltpu.VMEM)
    inputs = [q, docs, *pieces] + ([] if first else list(state))
    blocks = sum(s[2] for s in sources)
    return pl.pallas_call(
        functools.partial(attend_kernel, heads, sources, first, last),
        out_shape=jax.ShapeDtypeStruct((rows, width), jnp.bfloat16) if last else states,
        in_specs=[pl.BlockSpec(memory_space=pltpu.SMEM)] + [vmem] * len(inputs),
        out_specs=vmem if last else (vmem, vmem),
        scratch_shapes=[pltpu.VMEM(s.shape, s.dtype) for s in states] if last else [],
        compiler_params=pltpu.CompilerParams(vmem_limit_bytes=40 << 20),
        cost_estimate=pl.CostEstimate(
            flops=blocks * heads * rows * 2 * rows * HD * 6,
            bytes_accessed=blocks * rows * HD * 8,
            transcendentals=blocks * heads * rows * 2 * rows,
        ),
    )(where, *inputs)


def around(value, axis, size, step):
    return lax.ppermute(value, axis, [(i, (i + step) % size) for i in range(size)])


def ring_over_y(attended):
    half = attended.shape[0] // 2
    pieces = [(0, attended)]
    left = right = attended
    for step in range(1, Y // 2):
        left = around(left, "y", Y, 1)
        right = around(right, "y", Y, -1)
        pieces += [(-step, left), (step, right)]
    far = (around(left[:half], "y", Y, 1), around(right[half:], "y", Y, -1))
    return pieces + [(Y // 2, far)]


def project_kernel(y_ref, *refs):
    pieces, (weight_ref, out_ref, block_ref, acc_ref) = refs[: Y + 1], refs[Y + 1 :]
    step = pl.program_id(0)
    half = block_ref.shape[0] // 2
    for at in range(Y - 1):

        @pl.when(step == at)
        def _(at=at):
            block_ref[...] = pieces[at][...]

    @pl.when(step == Y - 1)
    def _():
        block_ref[:half] = pieces[Y - 1][...]
        block_ref[half:] = pieces[Y][...]

    @pl.when(step == 0)
    def _():
        acc_ref[...] = jnp.zeros_like(acc_ref)

    for x in range(X):
        acc_ref[x] += jnp.dot(
            block_ref[...], weight_ref[0, x, 0], preferred_element_type=jnp.float32
        )

    @pl.when(step == Y - 1)
    def _():
        width = acc_ref.shape[2]
        part = out_ref.shape[1]
        for x in range(X):
            for t in range(ZH * Y):
                out_ref[t, :, x * width : (x + 1) * width] = acc_ref[
                    x, t * part : (t + 1) * part
                ].astype(jnp.bfloat16)


def project(y, pieces, weight):
    rows, depth = pieces[0][1].shape
    width = weight.shape[2]
    weight = weight.reshape(ZL, X, CORE, depth, width)
    offsets = [offset for offset, _ in pieces]
    blocks = [block for _, block in pieces[:-1]] + list(pieces[-1][1])

    def weight_at(step, y_ref):
        offset = jnp.int32(0)
        for at, value in enumerate(offsets):
            offset = jnp.where(step == at, value, offset)
        their_y = lax.rem(y_ref[0] + offset + Y, Y)
        return (their_y // CORE, 0, their_y % CORE, 0, 0)

    whole = pl.BlockSpec(memory_space=pltpu.VMEM)
    out = (ZH * Y, rows // (ZH * Y), X * width)
    return pl.pallas_call(
        project_kernel,
        grid_spec=pltpu.PrefetchScalarGridSpec(
            num_scalar_prefetch=1,
            grid=(Y,),
            in_specs=[whole] * len(blocks) + [pl.BlockSpec((1, X, 1, depth, width), weight_at)],
            out_specs=pl.BlockSpec(out, lambda step, y_ref: (0, 0, 0)),
            scratch_shapes=[
                pltpu.VMEM((rows, depth), jnp.bfloat16),
                pltpu.VMEM((X, rows, width), jnp.float32),
            ],
        ),
        out_shape=jax.ShapeDtypeStruct(out, jnp.bfloat16),
        compiler_params=pltpu.CompilerParams(
            vmem_limit_bytes=60 << 20, dimension_semantics=("arbitrary",)
        ),
        cost_estimate=pl.CostEstimate(
            flops=2 * Y * rows * depth * X * width,
            bytes_accessed=2 * (Y * depth * X * width + Y * rows * depth),
            transcendentals=0,
        ),
    )(y, *blocks, weight)


def collect_kernel(came_ref, out_ref):
    width = came_ref.shape[2] // X
    for y in range(Y):
        for x in range(X):
            columns = slice(x * width, (x + 1) * width)
            both = came_ref[y, :, columns].astype(jnp.float32) + came_ref[
                Y + y, :, columns
            ].astype(jnp.float32)
            block = ((y // CORE) * X + x) * CORE + y % CORE
            out_ref[:, block * width : (block + 1) * width] = both.astype(jnp.bfloat16)


def collect(came):
    vmem = pl.BlockSpec(memory_space=pltpu.VMEM)
    return pl.pallas_call(
        collect_kernel,
        out_shape=jax.ShapeDtypeStruct((came.shape[1], Y * came.shape[2]), jnp.bfloat16),
        in_specs=[vmem],
        out_specs=vmem,
    )(came)


def on_device(queries, key_rows, value_rows, documents, out_weight):
    rows = queries.shape[0]
    heads_here = queries.shape[1] // HD
    kv = lax.axis_index(TP) * heads_here // (HEADS // KV_HEADS)
    own_keys = lax.dynamic_slice_in_dim(key_rows, kv * HD, HD, 1)
    own_values = lax.dynamic_slice_in_dim(value_rows, kv * HD, HD, 1)
    swap = [(a * Y + b, b * Y + a) for a in range(ZL * CORE) for b in range(Y)]
    weight = lax.all_gather(lax.ppermute(out_weight, ("zl", "core", "y"), swap), CTX, axis=0)
    doc_rows = jnp.broadcast_to(documents.astype(jnp.bfloat16)[None, :], (PAD, rows))
    packed = jnp.concatenate(
        [jnp.concatenate([own_keys, own_values], axis=1), doc_rows], axis=0
    )
    where = jnp.stack([lax.axis_index(a) for a in CTX]).astype(jnp.int32)
    docs = jnp.broadcast_to(documents.astype(jnp.float32)[:, None], (rows, HD))

    mine = lax.all_gather(packed, "zl", axis=0)
    left = around(mine, "x", X, 1)
    right = around(mine, "x", X, -1)
    mine_other = around(mine, "core", CORE, 1)
    far_a = around(left[: ZL // 2], "x", X, 1)
    far_b = around(right[ZL // 2 :], "x", X, -1)
    left_other = around(left, "core", CORE, 1)
    right_other = around(right, "core", CORE, 1)
    far_a_other = around(far_a, "core", CORE, 1)
    far_b_other = around(far_b, "core", CORE, 1)

    state = attend(where, queries, docs, [mine, mine_other], [(0, 0, ZL)], None, False)
    state = attend(
        where,
        queries,
        docs,
        [left, left_other, right, right_other],
        [(X - 1, 0, ZL), (1, 0, ZL)],
        state,
        False,
    )
    attended = attend(
        where,
        queries,
        docs,
        [far_a, far_a_other, far_b, far_b_other],
        [(2, 0, ZL // 2), (2, ZL // 2, ZL // 2)],
        state,
        True,
    )
    pieces = ring_over_y(attended)
    y = lax.axis_index("y").astype(jnp.int32).reshape(1)
    terms = project(y, pieces, weight)
    came = lax.all_to_all(terms, TP, split_axis=0, concat_axis=0, tiled=True)
    return collect(came)


def solution(mesh):
    fine = Mesh(mesh.devices.reshape(ZL, X, CORE, ZH, Y), AXES)
    in_specs = (P(CTX, TP), P(CTX, None), P(CTX, None), P(CTX), P(TP, CTX))
    return jax.shard_map(
        on_device, mesh=fine, in_specs=in_specs, out_specs=P(CTX + TP, None), check_vma=False
    )
```

```python
import functools
import math

import jax
import jax.numpy as jnp
from jax import lax
from jax.experimental import pallas as pl
from jax.experimental.pallas import tpu as pltpu
from jax.sharding import Mesh, PartitionSpec as P

HEADS = 64
KV_HEADS = 8
HD = 128
ZL, X, CORE, ZH, Y = 4, 4, 2, 2, 8
AXES = ("zl", "x", "core", "zh", "y")
CTX = ("zl", "x", "core")
TP = ("zh", "y")
PAD = 8
NEG = -1e30
SCALE2 = math.log2(math.e) / math.sqrt(HD)


def attend_kernel(heads, sources, first, last, where_ref, q_ref, docs_ref, *refs):
    n = len(sources)
    pieces = refs[: 2 * n]
    refs = refs[2 * n :]
    if not first:
        m_in, acc_in = refs[:2]
        refs = refs[2:]
    if last:
        out_ref, m_ref, acc_ref = refs
    else:
        m_ref, acc_ref = refs
    rows = q_ref.shape[0]
    my_z, my_x, my_core = where_ref[0], where_ref[1], where_ref[2]
    my_block = my_z * X + my_x
    if first:
        m_ref[...] = jnp.full_like(m_ref, NEG)
        acc_ref[...] = jnp.zeros_like(acc_ref)
    else:
        m_ref[...] = m_in[...]
        acc_ref[...] = acc_in[...]
    q_docs = docs_ref[...]
    q_first, q_last = jnp.min(q_docs), jnp.max(q_docs)
    ones = jnp.ones((rows, HD), jnp.bfloat16)

    for at, (offset, z_from, z_count) in enumerate(sources):
        own, other = pieces[2 * at], pieces[2 * at + 1]
        their_x = lax.rem(my_x + offset, X)

        def block(z, carry, own=own, other=other, their_x=their_x, z_from=z_from):
            their_block = (z_from + z) * X + their_x
            docs_own = own[z, rows : rows + PAD, :].astype(jnp.float32)
            docs_other = other[z, rows : rows + PAD, :].astype(jnp.float32)
            k_first = jnp.min(jnp.minimum(docs_own, docs_other))
            k_last = jnp.max(jnp.maximum(docs_own, docs_other))
            needed = (their_block <= my_block) & (k_last >= q_first)
            whole = needed & (their_block < my_block) & (k_first >= q_last)

            def update(masked):
                if masked:
                    row = lax.broadcasted_iota(jnp.int32, (rows, rows), 0)
                    lane = lax.broadcasted_iota(jnp.int32, (rows, rows), 1)
                    q_pos = my_block * (2 * rows) + my_core * rows + row
                    k_pos = their_block * (2 * rows) + lane
                    allowed = []
                    for side, docs in ((my_core, docs_own), (1 - my_core, docs_other)):
                        same = jnp.broadcast_to(docs[:1], (rows, rows)) == jnp.concatenate(
                            [q_docs] * (rows // HD), axis=1
                        )
                        allowed.append(same & (k_pos + side * rows <= q_pos))
                values = [
                    jnp.concatenate([ref[z, :rows, HD:], ones], axis=1) for ref in (own, other)
                ]
                for h in range(heads):
                    q = q_ref[:, h * HD : (h + 1) * HD]
                    scores = [
                        lax.dot_general(
                            q,
                            ref[z, :rows, :HD],
                            (((1,), (1,)), ((), ())),
                            preferred_element_type=jnp.float32,
                        )
                        for ref in (own, other)
                    ]
                    if masked:
                        scores = [jnp.where(a, s, NEG) for a, s in zip(allowed, scores)]
                    old = m_ref[h]
                    top = jnp.max(jnp.maximum(scores[0], scores[1]), axis=1, keepdims=True)
                    new = jnp.maximum(old, top)
                    wide = jnp.concatenate([new] * (rows // HD), axis=1)
                    total = None
                    for side in range(2):
                        weights = jnp.exp2((scores[side] - wide) * SCALE2)
                        if masked:
                            weights = jnp.where(allowed[side], weights, 0.0)
                        term = jnp.dot(
                            weights.astype(jnp.bfloat16),
                            values[side],
                            preferred_element_type=jnp.float32,
                        )
                        total = term if total is None else total + term
                    keep = jnp.exp2((old - new) * SCALE2)
                    m_ref[h] = new
                    acc_ref[h] = acc_ref[h] * jnp.concatenate([keep, keep], axis=1) + total

            @pl.when(whole)
            def _():
                update(False)

            @pl.when(needed & jnp.logical_not(whole))
            def _():
                update(True)

            return carry

        lax.fori_loop(0, z_count, block, 0)

    if last:
        for h in range(heads):
            done = (acc_ref[h, :, :HD] / acc_ref[h, :, HD:]).astype(jnp.bfloat16)
            out_ref[:, h * HD : (h + 1) * HD] = done


def attend(where, q, docs, pieces, sources, state, last):
    rows, width = q.shape
    heads = width // HD
    first = state is None
    states = (
        jax.ShapeDtypeStruct((heads, rows, HD), jnp.float32),
        jax.ShapeDtypeStruct((heads, rows, 2 * HD), jnp.float32),
    )
    vmem = pl.BlockSpec(memory_space=pltpu.VMEM)
    inputs = [q, docs, *pieces] + ([] if first else list(state))
    blocks = sum(s[2] for s in sources)
    return pl.pallas_call(
        functools.partial(attend_kernel, heads, sources, first, last),
        out_shape=jax.ShapeDtypeStruct((rows, width), jnp.bfloat16) if last else states,
        in_specs=[pl.BlockSpec(memory_space=pltpu.SMEM)] + [vmem] * len(inputs),
        out_specs=vmem if last else (vmem, vmem),
        scratch_shapes=[pltpu.VMEM(s.shape, s.dtype) for s in states] if last else [],
        compiler_params=pltpu.CompilerParams(vmem_limit_bytes=40 << 20),
        cost_estimate=pl.CostEstimate(
            flops=blocks * heads * rows * 2 * rows * HD * 6,
            bytes_accessed=blocks * rows * HD * 8,
            transcendentals=blocks * heads * rows * 2 * rows,
        ),
    )(where, *inputs)


def around(value, axis, size, step):
    return lax.ppermute(value, axis, [(i, (i + step) % size) for i in range(size)])


def ring_over_y(attended):
    half = attended.shape[0] // 2
    pieces = [(0, attended)]
    left = right = attended
    for step in range(1, Y // 2):
        left = around(left, "y", Y, 1)
        right = around(right, "y", Y, -1)
        pieces += [(-step, left), (step, right)]
    far = (around(left[:half], "y", Y, 1), around(right[half:], "y", Y, -1))
    return pieces + [(Y // 2, far)]


def project_kernel(y_ref, *refs):
    pieces, (weight_ref, out_ref, block_ref, acc_ref) = refs[: Y + 1], refs[Y + 1 :]
    step = pl.program_id(0)
    half = block_ref.shape[0] // 2
    for at in range(Y - 1):

        @pl.when(step == at)
        def _(at=at):
            block_ref[...] = pieces[at][...]

    @pl.when(step == Y - 1)
    def _():
        block_ref[:half] = pieces[Y - 1][...]
        block_ref[half:] = pieces[Y][...]

    @pl.when(step == 0)
    def _():
        acc_ref[...] = jnp.zeros_like(acc_ref)

    for z in range(ZL):
        acc_ref[z] += jnp.dot(
            block_ref[...], weight_ref[z, 0, 0], preferred_element_type=jnp.float32
        )

    @pl.when(step == Y - 1)
    def _():
        width = acc_ref.shape[2]
        part = out_ref.shape[1]
        for z in range(ZL):
            for t in range(ZH * Y):
                out_ref[t, :, z * width : (z + 1) * width] = acc_ref[
                    z, t * part : (t + 1) * part
                ].astype(jnp.bfloat16)


def project(y, pieces, weight):
    rows, depth = pieces[0][1].shape
    width = weight.shape[2]
    weight = weight.reshape(ZL, X, CORE, depth, width)
    offsets = [offset for offset, _ in pieces]
    blocks = [block for _, block in pieces[:-1]] + list(pieces[-1][1])

    def weight_at(step, y_ref):
        offset = jnp.int32(0)
        for at, value in enumerate(offsets):
            offset = jnp.where(step == at, value, offset)
        their_y = lax.rem(y_ref[0] + offset + Y, Y)
        return (0, their_y // CORE, their_y % CORE, 0, 0)

    whole = pl.BlockSpec(memory_space=pltpu.VMEM)
    out = (ZH * Y, rows // (ZH * Y), ZL * width)
    return pl.pallas_call(
        project_kernel,
        grid_spec=pltpu.PrefetchScalarGridSpec(
            num_scalar_prefetch=1,
            grid=(Y,),
            in_specs=[whole] * len(blocks) + [pl.BlockSpec((ZL, 1, 1, depth, width), weight_at)],
            out_specs=pl.BlockSpec(out, lambda step, y_ref: (0, 0, 0)),
            scratch_shapes=[
                pltpu.VMEM((rows, depth), jnp.bfloat16),
                pltpu.VMEM((ZL, rows, width), jnp.float32),
            ],
        ),
        out_shape=jax.ShapeDtypeStruct(out, jnp.bfloat16),
        compiler_params=pltpu.CompilerParams(
            vmem_limit_bytes=60 << 20, dimension_semantics=("arbitrary",)
        ),
        cost_estimate=pl.CostEstimate(
            flops=2 * Y * rows * depth * ZL * width,
            bytes_accessed=2 * (Y * depth * ZL * width + Y * rows * depth),
            transcendentals=0,
        ),
    )(y, *blocks, weight)


def collect_kernel(came_ref, out_ref):
    width = came_ref.shape[2] // ZL
    for y in range(Y):
        for z in range(ZL):
            columns = slice(z * width, (z + 1) * width)
            both = came_ref[y, :, columns].astype(jnp.float32) + came_ref[
                Y + y, :, columns
            ].astype(jnp.float32)
            block = z * X * CORE + y
            out_ref[:, block * width : (block + 1) * width] = both.astype(jnp.bfloat16)


def collect(came):
    vmem = pl.BlockSpec(memory_space=pltpu.VMEM)
    return pl.pallas_call(
        collect_kernel,
        out_shape=jax.ShapeDtypeStruct((came.shape[1], Y * came.shape[2]), jnp.bfloat16),
        in_specs=[vmem],
        out_specs=vmem,
    )(came)


def on_device(queries, key_rows, value_rows, documents, out_weight):
    rows = queries.shape[0]
    heads_here = queries.shape[1] // HD
    kv = lax.axis_index(TP) * heads_here // (HEADS // KV_HEADS)
    own_keys = lax.dynamic_slice_in_dim(key_rows, kv * HD, HD, 1)
    own_values = lax.dynamic_slice_in_dim(value_rows, kv * HD, HD, 1)
    swap = [(a * Y + b, b * Y + a) for a in range(X * CORE) for b in range(Y)]
    weight = lax.all_gather(lax.ppermute(out_weight, ("x", "core", "y"), swap), CTX, axis=0)
    doc_rows = jnp.broadcast_to(documents.astype(jnp.bfloat16)[None, :], (PAD, rows))
    packed = jnp.concatenate(
        [jnp.concatenate([own_keys, own_values], axis=1), doc_rows], axis=0
    )
    where = jnp.stack([lax.axis_index(a) for a in CTX]).astype(jnp.int32)
    docs = jnp.broadcast_to(documents.astype(jnp.float32)[:, None], (rows, HD))

    mine = lax.all_gather(packed, "zl", axis=0)
    left = around(mine, "x", X, 1)
    right = around(mine, "x", X, -1)
    mine_other = around(mine, "core", CORE, 1)
    far_a = around(left[: ZL // 2], "x", X, 1)
    far_b = around(right[ZL // 2 :], "x", X, -1)
    left_other = around(left, "core", CORE, 1)
    right_other = around(right, "core", CORE, 1)
    far_a_other = around(far_a, "core", CORE, 1)
    far_b_other = around(far_b, "core", CORE, 1)

    state = attend(where, queries, docs, [mine, mine_other], [(0, 0, ZL)], None, False)
    state = attend(
        where,
        queries,
        docs,
        [left, left_other, right, right_other],
        [(X - 1, 0, ZL), (1, 0, ZL)],
        state,
        False,
    )
    attended = attend(
        where,
        queries,
        docs,
        [far_a, far_a_other, far_b, far_b_other],
        [(2, 0, ZL // 2), (2, ZL // 2, ZL // 2)],
        state,
        True,
    )
    pieces = ring_over_y(attended)
    y = lax.axis_index("y").astype(jnp.int32).reshape(1)
    terms = project(y, pieces, weight)
    came = lax.all_to_all(terms, TP, split_axis=0, concat_axis=0, tiled=True)
    return collect(came)


def solution(mesh):
    fine = Mesh(mesh.devices.reshape(ZL, X, CORE, ZH, Y), AXES)
    in_specs = (P(CTX, TP), P(CTX, None), P(CTX, None), P(CTX), P(TP, CTX))
    return jax.shard_map(
        on_device, mesh=fine, in_specs=in_specs, out_specs=P(CTX + TP, None), check_vma=False
    )
```

```python
import functools
import math

import jax
import jax.numpy as jnp
from jax import lax
from jax.experimental import pallas as pl
from jax.experimental.pallas import tpu as pltpu
from jax.sharding import Mesh, PartitionSpec as P

HEADS = 64
KV_HEADS = 8
HD = 128
ZL, X, CORE, ZH, Y = 4, 4, 2, 2, 8
AXES = ("zl", "x", "core", "zh", "y")
CTX = ("zl", "x", "core")
TP = ("zh", "y")
PAD = 8
NEG = -1e30
SCALE2 = math.log2(math.e) / math.sqrt(HD)


def attend_kernel(heads, sources, first, last, where_ref, q_ref, docs_ref, *refs):
    n = len(sources)
    pieces = refs[: 2 * n]
    refs = refs[2 * n :]
    if not first:
        m_in, acc_in = refs[:2]
        refs = refs[2:]
    if last:
        out_ref, m_ref, acc_ref = refs
    else:
        m_ref, acc_ref = refs
    rows = q_ref.shape[0]
    my_z, my_x, my_core = where_ref[0], where_ref[1], where_ref[2]
    my_block = my_z * X + my_x
    if first:
        m_ref[...] = jnp.full_like(m_ref, NEG)
        acc_ref[...] = jnp.zeros_like(acc_ref)
    else:
        m_ref[...] = m_in[...]
        acc_ref[...] = acc_in[...]
    q_docs = docs_ref[...]
    q_first, q_last = jnp.min(q_docs), jnp.max(q_docs)
    ones = jnp.ones((rows, HD), jnp.bfloat16)

    for at, (offset, z_from, z_count) in enumerate(sources):
        own, other = pieces[2 * at], pieces[2 * at + 1]
        their_x = lax.rem(my_x + offset, X)

        def block(z, carry, own=own, other=other, their_x=their_x, z_from=z_from):
            their_block = (z_from + z) * X + their_x
            docs_own = own[z, rows : rows + PAD, :].astype(jnp.float32)
            docs_other = other[z, rows : rows + PAD, :].astype(jnp.float32)
            k_first = jnp.min(jnp.minimum(docs_own, docs_other))
            k_last = jnp.max(jnp.maximum(docs_own, docs_other))
            needed = (their_block <= my_block) & (k_last >= q_first)
            whole = needed & (their_block < my_block) & (k_first >= q_last)

            def update(masked):
                if masked:
                    row = lax.broadcasted_iota(jnp.int32, (rows, rows), 0)
                    lane = lax.broadcasted_iota(jnp.int32, (rows, rows), 1)
                    q_pos = my_block * (2 * rows) + my_core * rows + row
                    k_pos = their_block * (2 * rows) + lane
                    allowed = []
                    for side, docs in ((my_core, docs_own), (1 - my_core, docs_other)):
                        same = jnp.broadcast_to(docs[:1], (rows, rows)) == jnp.concatenate(
                            [q_docs] * (rows // HD), axis=1
                        )
                        allowed.append(same & (k_pos + side * rows <= q_pos))
                values = [
                    jnp.concatenate([ref[z, :rows, HD:], ones], axis=1) for ref in (own, other)
                ]
                for h in range(heads):
                    q = q_ref[:, h * HD : (h + 1) * HD]
                    scores = [
                        lax.dot_general(
                            q,
                            ref[z, :rows, :HD],
                            (((1,), (1,)), ((), ())),
                            preferred_element_type=jnp.float32,
                        )
                        for ref in (own, other)
                    ]
                    if masked:
                        scores = [jnp.where(a, s, NEG) for a, s in zip(allowed, scores)]
                    old = m_ref[h]
                    top = jnp.max(jnp.maximum(scores[0], scores[1]), axis=1, keepdims=True)
                    new = jnp.maximum(old, top)
                    wide = jnp.concatenate([new] * (rows // HD), axis=1)
                    total = None
                    for side in range(2):
                        weights = jnp.exp2((scores[side] - wide) * SCALE2)
                        if masked:
                            weights = jnp.where(allowed[side], weights, 0.0)
                        term = jnp.dot(
                            weights.astype(jnp.bfloat16),
                            values[side],
                            preferred_element_type=jnp.float32,
                        )
                        total = term if total is None else total + term
                    keep = jnp.exp2((old - new) * SCALE2)
                    m_ref[h] = new
                    acc_ref[h] = acc_ref[h] * jnp.concatenate([keep, keep], axis=1) + total

            @pl.when(whole)
            def _():
                update(False)

            @pl.when(needed & jnp.logical_not(whole))
            def _():
                update(True)

            return carry

        lax.fori_loop(0, z_count, block, 0)

    if last:
        for h in range(heads):
            done = (acc_ref[h, :, :HD] / acc_ref[h, :, HD:]).astype(jnp.bfloat16)
            out_ref[:, h * HD : (h + 1) * HD] = done


def attend(where, q, docs, pieces, sources, state, last):
    rows, width = q.shape
    heads = width // HD
    first = state is None
    states = (
        jax.ShapeDtypeStruct((heads, rows, HD), jnp.float32),
        jax.ShapeDtypeStruct((heads, rows, 2 * HD), jnp.float32),
    )
    vmem = pl.BlockSpec(memory_space=pltpu.VMEM)
    inputs = [q, docs, *pieces] + ([] if first else list(state))
    blocks = sum(s[2] for s in sources)
    return pl.pallas_call(
        functools.partial(attend_kernel, heads, sources, first, last),
        out_shape=jax.ShapeDtypeStruct((rows, width), jnp.bfloat16) if last else states,
        in_specs=[pl.BlockSpec(memory_space=pltpu.SMEM)] + [vmem] * len(inputs),
        out_specs=vmem if last else (vmem, vmem),
        scratch_shapes=[pltpu.VMEM(s.shape, s.dtype) for s in states] if last else [],
        compiler_params=pltpu.CompilerParams(vmem_limit_bytes=40 << 20),
        cost_estimate=pl.CostEstimate(
            flops=blocks * heads * rows * 2 * rows * HD * 6,
            bytes_accessed=blocks * rows * HD * 8,
            transcendentals=blocks * heads * rows * 2 * rows,
        ),
    )(where, *inputs)


def around(value, axis, size, step):
    return lax.ppermute(value, axis, [(i, (i + step) % size) for i in range(size)])


def ring_over_y(attended):
    half = attended.shape[0] // 2
    pieces = [(0, attended)]
    left = right = attended
    for step in range(1, Y // 2):
        left = around(left, "y", Y, 1)
        right = around(right, "y", Y, -1)
        pieces += [(-step, left), (step, right)]
    far = (around(left[:half], "y", Y, 1), around(right[half:], "y", Y, -1))
    return pieces + [(Y // 2, far)]


def project_kernel(offsets, y_ref, *refs):
    pieces, (weight_ref, out_ref, held_ref, acc_ref, sems) = refs[: Y + 1], refs[Y + 1 :]
    half = acc_ref.shape[1] // 2
    width = acc_ref.shape[2]
    part = out_ref.shape[1]

    def copy(at, z):
        their_y = lax.rem(y_ref[0] + (offsets[at] + Y), Y)
        return pltpu.make_async_copy(
            weight_ref.at[z, their_y], held_ref.at[at, z], sems.at[at, z]
        )

    for at in range(Y):
        for z in range(ZL):
            copy(at, z).start()
    for at in range(Y):
        for z in range(ZL):
            copy(at, z).wait()
            if at < Y - 1:
                term = jnp.dot(
                    pieces[at][...], held_ref[at, z], preferred_element_type=jnp.float32
                )
                acc_ref[z] = term if at == 0 else acc_ref[z] + term
                continue
            for side in range(2):
                rows = slice(side * half, (side + 1) * half)
                term = jnp.dot(
                    pieces[at + side][...], held_ref[at, z], preferred_element_type=jnp.float32
                )
                done = (acc_ref[z, rows] + term).astype(jnp.bfloat16)
                out_ref[
                    side * half // part : (side + 1) * half // part,
                    :,
                    z * width : (z + 1) * width,
                ] = done.reshape(half // part, part, width)


def project(y, pieces, weight):
    rows, depth = pieces[0][1].shape
    width = weight.shape[2]
    weight = weight.reshape(ZL, X * CORE, depth, width)
    offsets = tuple(offset for offset, _ in pieces)
    blocks = [block for _, block in pieces[:-1]] + list(pieces[-1][1])
    whole = pl.BlockSpec(memory_space=pltpu.VMEM)
    out = (ZH * Y, rows // (ZH * Y), ZL * width)
    return pl.pallas_call(
        functools.partial(project_kernel, offsets),
        out_shape=jax.ShapeDtypeStruct(out, jnp.bfloat16),
        in_specs=[pl.BlockSpec(memory_space=pltpu.SMEM)]
        + [whole] * len(blocks)
        + [pl.BlockSpec(memory_space=pltpu.HBM)],
        out_specs=whole,
        scratch_shapes=[
            pltpu.VMEM((Y, ZL, depth, width), jnp.bfloat16),
            pltpu.VMEM((ZL, rows, width), jnp.float32),
            pltpu.SemaphoreType.DMA((Y, ZL)),
        ],
        compiler_params=pltpu.CompilerParams(vmem_limit_bytes=24 << 20),
        cost_estimate=pl.CostEstimate(
            flops=2 * Y * rows * depth * ZL * width,
            bytes_accessed=2 * (Y * depth * ZL * width + Y * rows * depth),
            transcendentals=0,
        ),
    )(y, *blocks, weight)


def collect_kernel(came_ref, out_ref):
    width = came_ref.shape[2] // ZL
    for y in range(Y):
        for z in range(ZL):
            columns = slice(z * width, (z + 1) * width)
            both = came_ref[y, :, columns].astype(jnp.float32) + came_ref[
                Y + y, :, columns
            ].astype(jnp.float32)
            block = z * X * CORE + y
            out_ref[:, block * width : (block + 1) * width] = both.astype(jnp.bfloat16)


def collect(came):
    vmem = pl.BlockSpec(memory_space=pltpu.VMEM)
    return pl.pallas_call(
        collect_kernel,
        out_shape=jax.ShapeDtypeStruct((came.shape[1], Y * came.shape[2]), jnp.bfloat16),
        in_specs=[vmem],
        out_specs=vmem,
    )(came)


def compute(queries, key_rows, value_rows, documents, out_weight):
    rows = queries.shape[0]
    heads_here = queries.shape[1] // HD
    swap = [(a * Y + b, b * Y + a) for a in range(X * CORE) for b in range(Y)]
    swapped = lax.ppermute(out_weight, ("x", "core", "y"), swap)
    weight = lax.all_gather(swapped, CTX, axis=0)

    kv = lax.axis_index(TP) * heads_here // (HEADS // KV_HEADS)
    own_keys = lax.dynamic_slice_in_dim(key_rows, kv * HD, HD, 1)
    own_values = lax.dynamic_slice_in_dim(value_rows, kv * HD, HD, 1)
    doc_rows = jnp.broadcast_to(documents.astype(jnp.bfloat16)[None, :], (PAD, rows))
    packed = jnp.concatenate(
        [jnp.concatenate([own_keys, own_values], axis=1), doc_rows], axis=0
    )
    where = jnp.stack([lax.axis_index(a) for a in CTX]).astype(jnp.int32)
    docs = jnp.broadcast_to(documents.astype(jnp.float32)[:, None], (rows, HD))

    mine = lax.all_gather(packed, "zl", axis=0)
    left = around(mine, "x", X, 1)
    right = around(mine, "x", X, -1)
    mine_other = around(mine, "core", CORE, 1)
    far_a = around(left[: ZL // 2], "x", X, 1)
    far_b = around(right[ZL // 2 :], "x", X, -1)
    left_other = around(left, "core", CORE, 1)
    right_other = around(right, "core", CORE, 1)
    far = jnp.concatenate([far_a, far_b], axis=0)
    far_other = around(far, "core", CORE, 1)

    state = attend(where, queries, docs, [mine, mine_other], [(0, 0, ZL)], None, False)
    state = attend(
        where,
        queries,
        docs,
        [left, left_other, right, right_other],
        [(X - 1, 0, ZL), (1, 0, ZL)],
        state,
        False,
    )
    attended = attend(where, queries, docs, [far, far_other], [(2, 0, ZL)], state, True)
    pieces = ring_over_y(attended)
    y = lax.axis_index("y").astype(jnp.int32).reshape(1)
    terms = project(y, pieces, weight)
    came = lax.all_to_all(terms, TP, split_axis=0, concat_axis=0, tiled=True)
    return collect(came)


def solution(mesh):
    fine = Mesh(mesh.devices.reshape(ZL, X, CORE, ZH, Y), AXES)
    in_specs = (P(CTX, TP), P(CTX, None), P(CTX, None), P(CTX), P(TP, CTX))
    return jax.shard_map(
        compute, mesh=fine, in_specs=in_specs, out_specs=P(CTX + TP, None), check_vma=False
    )
```

```python
import functools
import math

import jax
import jax.numpy as jnp
from jax import lax
from jax.experimental import pallas as pl
from jax.experimental.pallas import tpu as pltpu
from jax.sharding import Mesh, PartitionSpec as P

HEADS = 64
KV_HEADS = 8
HD = 128
ZL, X, CORE, ZH, Y = 4, 4, 2, 2, 8
AXES = ("zl", "x", "core", "zh", "y")
CTX = ("zl", "x", "core")
TP = ("zh", "y")
PAD = 8
GROUP = 1
NEG = -1e30
SCALE2 = math.log2(math.e) / math.sqrt(HD)


def attend_kernel(group, sources, first, last, where_ref, q_ref, docs_ref, *refs):
    n = len(sources)
    pieces = refs[: 2 * n]
    refs = refs[2 * n :]
    if not first:
        m_in, acc_in = refs[:2]
        refs = refs[2:]
    if last:
        out_ref, m_ref, acc_ref, stack_ref = refs
    else:
        m_ref, acc_ref, stack_ref = refs
    rows = q_ref.shape[0]
    heads = q_ref.shape[1] // HD
    my_z, my_x, my_core = where_ref[0], where_ref[1], where_ref[2]
    my_block = my_z * X + my_x
    if first:
        m_ref[...] = jnp.full_like(m_ref, NEG)
        acc_ref[...] = jnp.zeros_like(acc_ref)
    else:
        m_ref[...] = m_in[...]
        acc_ref[...] = acc_in[...]
    for h in range(heads):
        stack_ref[h * rows : (h + 1) * rows, :] = q_ref[:, h * HD : (h + 1) * HD]
    q_docs = docs_ref[...]
    q_first, q_last = jnp.min(q_docs), jnp.max(q_docs)
    ones = jnp.ones((rows, HD), jnp.bfloat16)
    wide = rows // HD

    for at, offset in enumerate(sources):
        own, other = pieces[2 * at], pieces[2 * at + 1]
        their_x = lax.rem(my_x + offset, X)

        def block(z, carry, own=own, other=other, their_x=their_x):
            their_block = z * X + their_x
            docs_own = own[z, rows : rows + PAD, :].astype(jnp.float32)
            docs_other = other[z, rows : rows + PAD, :].astype(jnp.float32)
            k_first = jnp.min(jnp.minimum(docs_own, docs_other))
            k_last = jnp.max(jnp.maximum(docs_own, docs_other))
            needed = (their_block <= my_block) & (k_last >= q_first)
            whole = needed & (their_block < my_block) & (k_first >= q_last)

            def update(masked):
                if masked:
                    row = lax.broadcasted_iota(jnp.int32, (rows, rows), 0)
                    lane = lax.broadcasted_iota(jnp.int32, (rows, rows), 1)
                    q_pos = my_block * (2 * rows) + my_core * rows + row
                    k_pos = their_block * (2 * rows) + lane
                    allowed = []
                    for side, docs in ((my_core, docs_own), (1 - my_core, docs_other)):
                        same = jnp.broadcast_to(docs[:1], (rows, rows)) == jnp.concatenate(
                            [q_docs] * wide, axis=1
                        )
                        one = same & (k_pos + side * rows <= q_pos)
                        one = jnp.where(one, 1.0, 0.0)
                        allowed.append(jnp.concatenate([one] * group, axis=0) > 0.5)
                keys = [ref[z, :rows, :HD] for ref in (own, other)]
                values = [
                    jnp.concatenate([ref[z, :rows, HD:], ones], axis=1) for ref in (own, other)
                ]
                for g in range(heads // group):
                    these = slice(g * group * rows, (g + 1) * group * rows)
                    q = stack_ref[these, :]
                    scores = [
                        lax.dot_general(
                            q, k, (((1,), (1,)), ((), ())), preferred_element_type=jnp.float32
                        )
                        for k in keys
                    ]
                    if masked:
                        scores = [jnp.where(a, s, NEG) for a, s in zip(allowed, scores)]
                    old = m_ref[these, :]
                    top = jnp.max(jnp.maximum(scores[0], scores[1]), axis=1, keepdims=True)
                    new = jnp.maximum(old, top)
                    broad = jnp.concatenate([new] * wide, axis=1)
                    total = None
                    for side in range(2):
                        weights = jnp.exp2((scores[side] - broad) * SCALE2)
                        if masked:
                            weights = jnp.where(allowed[side], weights, 0.0)
                        term = jnp.dot(
                            weights.astype(jnp.bfloat16),
                            values[side],
                            preferred_element_type=jnp.float32,
                        )
                        total = term if total is None else total + term
                    keep = jnp.exp2((old - new) * SCALE2)
                    m_ref[these, :] = new
                    acc_ref[these, :] = (
                        acc_ref[these, :] * jnp.concatenate([keep, keep], axis=1) + total
                    )

            @pl.when(whole)
            def _():
                update(False)

            @pl.when(needed & jnp.logical_not(whole))
            def _():
                update(True)

            return carry

        lax.fori_loop(0, ZL, block, 0)

    if last:
        for h in range(heads):
            these = slice(h * rows, (h + 1) * rows)
            out_ref[:, h * HD : (h + 1) * HD] = (
                acc_ref[these, :HD] / acc_ref[these, HD:]
            ).astype(jnp.bfloat16)


def attend(where, q, docs, pieces, sources, state, last, group=GROUP):
    rows, width = q.shape
    heads = width // HD
    first = state is None
    states = (
        jax.ShapeDtypeStruct((heads * rows, HD), jnp.float32),
        jax.ShapeDtypeStruct((heads * rows, 2 * HD), jnp.float32),
    )
    vmem = pl.BlockSpec(memory_space=pltpu.VMEM)
    inputs = [q, docs, *pieces] + ([] if first else list(state))
    blocks = ZL * len(sources)
    return pl.pallas_call(
        functools.partial(attend_kernel, group, sources, first, last),
        out_shape=jax.ShapeDtypeStruct((rows, width), jnp.bfloat16) if last else states,
        in_specs=[pl.BlockSpec(memory_space=pltpu.SMEM)] + [vmem] * len(inputs),
        out_specs=vmem if last else (vmem, vmem),
        scratch_shapes=([pltpu.VMEM(s.shape, s.dtype) for s in states] if last else [])
        + [pltpu.VMEM((heads * rows, HD), jnp.bfloat16)],
        compiler_params=pltpu.CompilerParams(vmem_limit_bytes=40 << 20),
        cost_estimate=pl.CostEstimate(
            flops=blocks * heads * rows * 2 * rows * HD * 6,
            bytes_accessed=blocks * rows * HD * 8,
            transcendentals=blocks * heads * rows * 2 * rows,
        ),
    )(where, *inputs)


def around(value, axis, size, step):
    return lax.ppermute(value, axis, [(i, (i + step) % size) for i in range(size)])


def ring_over_y(attended):
    half = attended.shape[0] // 2
    pieces = [(0, attended)]
    left = right = attended
    for step in range(1, Y // 2):
        left = around(left, "y", Y, 1)
        right = around(right, "y", Y, -1)
        pieces += [(-step, left), (step, right)]
    far = (around(left[:half], "y", Y, 1), around(right[half:], "y", Y, -1))
    return pieces + [(Y // 2, far)]


def project_kernel(offsets, y_ref, *refs):
    pieces, (weight_ref, out_ref, held_ref, acc_ref, sems) = refs[: Y + 1], refs[Y + 1 :]
    half = acc_ref.shape[1] // 2
    width = acc_ref.shape[2]
    part = out_ref.shape[1]

    def copy(at, z):
        their_y = lax.rem(y_ref[0] + (offsets[at] + Y), Y)
        return pltpu.make_async_copy(
            weight_ref.at[z, their_y], held_ref.at[at, z], sems.at[at, z]
        )

    for at in range(Y):
        for z in range(ZL):
            copy(at, z).start()
    for at in range(Y):
        for z in range(ZL):
            copy(at, z).wait()
            if at < Y - 1:
                term = jnp.dot(
                    pieces[at][...], held_ref[at, z], preferred_element_type=jnp.float32
                )
                acc_ref[z] = term if at == 0 else acc_ref[z] + term
                continue
            for side in range(2):
                rows = slice(side * half, (side + 1) * half)
                term = jnp.dot(
                    pieces[at + side][...], held_ref[at, z], preferred_element_type=jnp.float32
                )
                done = (acc_ref[z, rows] + term).astype(jnp.bfloat16)
                out_ref[
                    side * half // part : (side + 1) * half // part,
                    :,
                    z * width : (z + 1) * width,
                ] = done.reshape(half // part, part, width)


def project(y, pieces, weight):
    rows, depth = pieces[0][1].shape
    width = weight.shape[2]
    weight = weight.reshape(ZL, X * CORE, depth, width)
    offsets = tuple(offset for offset, _ in pieces)
    blocks = [block for _, block in pieces[:-1]] + list(pieces[-1][1])
    whole = pl.BlockSpec(memory_space=pltpu.VMEM)
    out = (ZH * Y, rows // (ZH * Y), ZL * width)
    return pl.pallas_call(
        functools.partial(project_kernel, offsets),
        out_shape=jax.ShapeDtypeStruct(out, jnp.bfloat16),
        in_specs=[pl.BlockSpec(memory_space=pltpu.SMEM)]
        + [whole] * len(blocks)
        + [pl.BlockSpec(memory_space=pltpu.HBM)],
        out_specs=whole,
        scratch_shapes=[
            pltpu.VMEM((Y, ZL, depth, width), jnp.bfloat16),
            pltpu.VMEM((ZL, rows, width), jnp.float32),
            pltpu.SemaphoreType.DMA((Y, ZL)),
        ],
        compiler_params=pltpu.CompilerParams(vmem_limit_bytes=24 << 20),
        cost_estimate=pl.CostEstimate(
            flops=2 * Y * rows * depth * ZL * width,
            bytes_accessed=2 * (Y * depth * ZL * width + Y * rows * depth),
            transcendentals=0,
        ),
    )(y, *blocks, weight)


def collect_kernel(came_ref, out_ref):
    width = came_ref.shape[2] // ZL
    for y in range(Y):
        for z in range(ZL):
            columns = slice(z * width, (z + 1) * width)
            both = came_ref[y, :, columns].astype(jnp.float32) + came_ref[
                Y + y, :, columns
            ].astype(jnp.float32)
            block = z * X * CORE + y
            out_ref[:, block * width : (block + 1) * width] = both.astype(jnp.bfloat16)


def collect(came):
    vmem = pl.BlockSpec(memory_space=pltpu.VMEM)
    return pl.pallas_call(
        collect_kernel,
        out_shape=jax.ShapeDtypeStruct((came.shape[1], Y * came.shape[2]), jnp.bfloat16),
        in_specs=[vmem],
        out_specs=vmem,
    )(came)


def compute(queries, key_rows, value_rows, documents, out_weight):
    rows = queries.shape[0]
    heads_here = queries.shape[1] // HD
    swap = [(a * Y + b, b * Y + a) for a in range(X * CORE) for b in range(Y)]
    swapped = lax.ppermute(out_weight, ("x", "core", "y"), swap)
    weight = lax.all_gather(swapped, CTX, axis=0)

    kv = lax.axis_index(TP) * heads_here // (HEADS // KV_HEADS)
    own_keys = lax.dynamic_slice_in_dim(key_rows, kv * HD, HD, 1)
    own_values = lax.dynamic_slice_in_dim(value_rows, kv * HD, HD, 1)
    doc_rows = jnp.broadcast_to(documents.astype(jnp.bfloat16)[None, :], (PAD, rows))
    packed = jnp.concatenate(
        [jnp.concatenate([own_keys, own_values], axis=1), doc_rows], axis=0
    )
    where = jnp.stack([lax.axis_index(a) for a in CTX]).astype(jnp.int32)
    docs = jnp.broadcast_to(documents.astype(jnp.float32)[:, None], (rows, HD))

    mine = lax.all_gather(packed, "zl", axis=0)
    left = around(mine, "x", X, 1)
    right = around(mine, "x", X, -1)
    mine_other = around(mine, "core", CORE, 1)
    far_a = around(left[: ZL // 2], "x", X, 1)
    far_b = around(right[ZL // 2 :], "x", X, -1)
    left_other = around(left, "core", CORE, 1)
    right_other = around(right, "core", CORE, 1)
    far = jnp.concatenate([far_a, far_b], axis=0)
    far_other = around(far, "core", CORE, 1)

    state = attend(where, queries, docs, [mine, mine_other], (0,), None, False)
    state = attend(where, queries, docs, [left, left_other], (X - 1,), state, False)
    state = attend(where, queries, docs, [right, right_other], (1,), state, False)
    attended = attend(where, queries, docs, [far, far_other], (2,), state, True)
    pieces = ring_over_y(attended)
    y = lax.axis_index("y").astype(jnp.int32).reshape(1)
    terms = project(y, pieces, weight)
    came = lax.all_to_all(terms, TP, split_axis=0, concat_axis=0, tiled=True)
    return collect(came)


def solution(mesh):
    fine = Mesh(mesh.devices.reshape(ZL, X, CORE, ZH, Y), AXES)
    in_specs = (P(CTX, TP), P(CTX, None), P(CTX, None), P(CTX), P(TP, CTX))
    return jax.shard_map(
        compute, mesh=fine, in_specs=in_specs, out_specs=P(CTX + TP, None), check_vma=False
    )
```

```python
import functools
import math

import jax
import jax.numpy as jnp
from jax import lax
from jax.experimental import pallas as pl
from jax.experimental.pallas import tpu as pltpu
from jax.sharding import Mesh, PartitionSpec as P

HEADS = 64
KV_HEADS = 8
HD = 128
ZL, X, CORE, ZH, Y = 4, 4, 2, 2, 8
AXES = ("zl", "x", "core", "zh", "y")
CTX = ("zl", "x", "core")
TP = ("zh", "y")
PAD = 8
GROUP = 1
NEG = -1e30
SCALE2 = math.log2(math.e) / math.sqrt(HD)


def attend_kernel(group, sources, first, last, where_ref, q_ref, docs_ref, *refs):
    n = len(sources)
    pieces = refs[: 2 * n]
    refs = refs[2 * n :]
    if not first:
        m_in, acc_in = refs[:2]
        refs = refs[2:]
    if last:
        out_ref, m_ref, acc_ref, stack_ref = refs
    else:
        m_ref, acc_ref, stack_ref = refs
    rows = q_ref.shape[0]
    heads = q_ref.shape[1] // HD
    my_z, my_x, my_core = where_ref[0], where_ref[1], where_ref[2]
    my_block = my_z * X + my_x
    if first:
        m_ref[...] = jnp.full_like(m_ref, NEG)
        acc_ref[...] = jnp.zeros_like(acc_ref)
    else:
        m_ref[...] = m_in[...]
        acc_ref[...] = acc_in[...]
    for h in range(heads):
        stack_ref[h * rows : (h + 1) * rows, :] = q_ref[:, h * HD : (h + 1) * HD]
    q_docs = docs_ref[...]
    q_first, q_last = jnp.min(q_docs), jnp.max(q_docs)
    ones = jnp.ones((rows, HD), jnp.bfloat16)
    wide = rows // HD

    for at, offset in enumerate(sources):
        own, other = pieces[2 * at], pieces[2 * at + 1]
        their_x = lax.rem(my_x + offset, X)

        def block(z, carry, own=own, other=other, their_x=their_x):
            their_block = z * X + their_x
            docs_own = own[z, rows : rows + PAD, :].astype(jnp.float32)
            docs_other = other[z, rows : rows + PAD, :].astype(jnp.float32)
            k_first = jnp.min(jnp.minimum(docs_own, docs_other))
            k_last = jnp.max(jnp.maximum(docs_own, docs_other))
            needed = (their_block <= my_block) & (k_last >= q_first)
            whole = needed & (their_block < my_block) & (k_first >= q_last)

            def update(masked):
                if masked:
                    row = lax.broadcasted_iota(jnp.int32, (rows, rows), 0)
                    lane = lax.broadcasted_iota(jnp.int32, (rows, rows), 1)
                    q_pos = my_block * (2 * rows) + my_core * rows + row
                    k_pos = their_block * (2 * rows) + lane
                    allowed = []
                    for side, docs in ((my_core, docs_own), (1 - my_core, docs_other)):
                        same = jnp.broadcast_to(docs[:1], (rows, rows)) == jnp.concatenate(
                            [q_docs] * wide, axis=1
                        )
                        one = same & (k_pos + side * rows <= q_pos)
                        one = jnp.where(one, 1.0, 0.0)
                        allowed.append(jnp.concatenate([one] * group, axis=0) > 0.5)
                keys = [ref[z, :rows, :HD] for ref in (own, other)]
                values = [
                    jnp.concatenate([ref[z, :rows, HD:], ones], axis=1) for ref in (own, other)
                ]
                for g in range(heads // group):
                    these = slice(g * group * rows, (g + 1) * group * rows)
                    q = stack_ref[these, :]
                    scores = [
                        lax.dot_general(
                            q, k, (((1,), (1,)), ((), ())), preferred_element_type=jnp.float32
                        )
                        for k in keys
                    ]
                    if masked:
                        scores = [jnp.where(a, s, NEG) for a, s in zip(allowed, scores)]
                    old = m_ref[these, :]
                    top = jnp.max(jnp.maximum(scores[0], scores[1]), axis=1, keepdims=True)
                    new = jnp.maximum(old, top)
                    broad = jnp.concatenate([new] * wide, axis=1)
                    total = None
                    for side in range(2):
                        weights = jnp.exp2((scores[side] - broad) * SCALE2)
                        if masked:
                            weights = jnp.where(allowed[side], weights, 0.0)
                        term = jnp.dot(
                            weights.astype(jnp.bfloat16),
                            values[side],
                            preferred_element_type=jnp.float32,
                        )
                        total = term if total is None else total + term
                    keep = jnp.exp2((old - new) * SCALE2)
                    m_ref[these, :] = new
                    acc_ref[these, :] = (
                        acc_ref[these, :] * jnp.concatenate([keep, keep], axis=1) + total
                    )

            @pl.when(whole)
            def _():
                update(False)

            @pl.when(needed & jnp.logical_not(whole))
            def _():
                update(True)

            return carry

        lax.fori_loop(0, ZL, block, 0)

    if last:
        for h in range(heads):
            these = slice(h * rows, (h + 1) * rows)
            out_ref[:, h * HD : (h + 1) * HD] = (
                acc_ref[these, :HD] / acc_ref[these, HD:]
            ).astype(jnp.bfloat16)


def attend(where, q, docs, pieces, sources, state, last, group=GROUP):
    rows, width = q.shape
    heads = width // HD
    first = state is None
    states = (
        jax.ShapeDtypeStruct((heads * rows, HD), jnp.float32),
        jax.ShapeDtypeStruct((heads * rows, 2 * HD), jnp.float32),
    )
    vmem = pl.BlockSpec(memory_space=pltpu.VMEM)
    inputs = [q, docs, *pieces] + ([] if first else list(state))
    blocks = ZL * len(sources)
    return pl.pallas_call(
        functools.partial(attend_kernel, group, sources, first, last),
        out_shape=jax.ShapeDtypeStruct((rows, width), jnp.bfloat16) if last else states,
        in_specs=[pl.BlockSpec(memory_space=pltpu.SMEM)] + [vmem] * len(inputs),
        out_specs=vmem if last else (vmem, vmem),
        scratch_shapes=([pltpu.VMEM(s.shape, s.dtype) for s in states] if last else [])
        + [pltpu.VMEM((heads * rows, HD), jnp.bfloat16)],
        compiler_params=pltpu.CompilerParams(vmem_limit_bytes=40 << 20),
        cost_estimate=pl.CostEstimate(
            flops=blocks * heads * rows * 2 * rows * HD * 6,
            bytes_accessed=blocks * rows * HD * 8,
            transcendentals=blocks * heads * rows * 2 * rows,
        ),
    )(where, *inputs)


def around(value, axis, size, step):
    return lax.ppermute(value, axis, [(i, (i + step) % size) for i in range(size)])


def ring_over_y(attended):
    half = attended.shape[0] // 2
    pieces = [(0, attended)]
    left = right = attended
    for step in range(1, Y // 2):
        if step == Y // 2 - 1:
            far = (around(left[:half], "y", Y, 2), around(right[half:], "y", Y, -2))
        left = around(left, "y", Y, 1)
        right = around(right, "y", Y, -1)
        pieces += [(-step, left), (step, right)]
    return pieces + [(Y // 2, far)]


def project_kernel(offsets, y_ref, *refs):
    pieces, (weight_ref, out_ref, held_ref, acc_ref, sems) = refs[: Y + 1], refs[Y + 1 :]
    half = acc_ref.shape[1] // 2
    width = acc_ref.shape[2]
    part = out_ref.shape[1]

    def copy(at, z):
        their_y = lax.rem(y_ref[0] + (offsets[at] + Y), Y)
        return pltpu.make_async_copy(
            weight_ref.at[z, their_y], held_ref.at[at, z], sems.at[at, z]
        )

    for at in range(Y):
        for z in range(ZL):
            copy(at, z).start()
    for at in range(Y):
        for z in range(ZL):
            copy(at, z).wait()
            if at < Y - 1:
                term = jnp.dot(
                    pieces[at][...], held_ref[at, z], preferred_element_type=jnp.float32
                )
                acc_ref[z] = term if at == 0 else acc_ref[z] + term
                continue
            for side in range(2):
                rows = slice(side * half, (side + 1) * half)
                term = jnp.dot(
                    pieces[at + side][...], held_ref[at, z], preferred_element_type=jnp.float32
                )
                done = (acc_ref[z, rows] + term).astype(jnp.bfloat16)
                out_ref[
                    side * half // part : (side + 1) * half // part,
                    :,
                    z * width : (z + 1) * width,
                ] = done.reshape(half // part, part, width)


def project(y, pieces, weight):
    rows, depth = pieces[0][1].shape
    width = weight.shape[2]
    weight = weight.reshape(ZL, X * CORE, depth, width)
    offsets = tuple(offset for offset, _ in pieces)
    blocks = [block for _, block in pieces[:-1]] + list(pieces[-1][1])
    whole = pl.BlockSpec(memory_space=pltpu.VMEM)
    out = (ZH * Y, rows // (ZH * Y), ZL * width)
    return pl.pallas_call(
        functools.partial(project_kernel, offsets),
        out_shape=jax.ShapeDtypeStruct(out, jnp.bfloat16),
        in_specs=[pl.BlockSpec(memory_space=pltpu.SMEM)]
        + [whole] * len(blocks)
        + [pl.BlockSpec(memory_space=pltpu.HBM)],
        out_specs=whole,
        scratch_shapes=[
            pltpu.VMEM((Y, ZL, depth, width), jnp.bfloat16),
            pltpu.VMEM((ZL, rows, width), jnp.float32),
            pltpu.SemaphoreType.DMA((Y, ZL)),
        ],
        compiler_params=pltpu.CompilerParams(vmem_limit_bytes=51 << 20),
        cost_estimate=pl.CostEstimate(
            flops=2 * Y * rows * depth * ZL * width,
            bytes_accessed=2 * (Y * depth * ZL * width + Y * rows * depth),
            transcendentals=0,
        ),
    )(y, *blocks, weight)


def collect_kernel(came_ref, out_ref):
    width = came_ref.shape[2] // ZL
    for y in range(Y):
        for z in range(ZL):
            columns = slice(z * width, (z + 1) * width)
            both = came_ref[y, :, columns].astype(jnp.float32) + came_ref[
                Y + y, :, columns
            ].astype(jnp.float32)
            block = z * X * CORE + y
            out_ref[:, block * width : (block + 1) * width] = both.astype(jnp.bfloat16)


def collect(came):
    vmem = pl.BlockSpec(memory_space=pltpu.VMEM)
    return pl.pallas_call(
        collect_kernel,
        out_shape=jax.ShapeDtypeStruct((came.shape[1], Y * came.shape[2]), jnp.bfloat16),
        in_specs=[vmem],
        out_specs=vmem,
    )(came)


def compute(queries, key_rows, value_rows, documents, out_weight):
    rows = queries.shape[0]
    heads_here = queries.shape[1] // HD
    swap = [(a * Y + b, b * Y + a) for a in range(X * CORE) for b in range(Y)]
    swapped = lax.ppermute(out_weight, ("x", "core", "y"), swap)
    weight = lax.all_gather(swapped, CTX, axis=0)

    kv = lax.axis_index(TP) * heads_here // (HEADS // KV_HEADS)
    own_keys = lax.dynamic_slice_in_dim(key_rows, kv * HD, HD, 1)
    own_values = lax.dynamic_slice_in_dim(value_rows, kv * HD, HD, 1)
    doc_rows = jnp.broadcast_to(documents.astype(jnp.bfloat16)[None, :], (PAD, rows))
    packed = jnp.concatenate(
        [jnp.concatenate([own_keys, own_values], axis=1), doc_rows], axis=0
    )
    where = jnp.stack([lax.axis_index(a) for a in CTX]).astype(jnp.int32)
    docs = jnp.broadcast_to(documents.astype(jnp.float32)[:, None], (rows, HD))

    mine = lax.all_gather(packed, "zl", axis=0)
    left = around(mine, "x", X, 1)
    right = around(mine, "x", X, -1)
    mine_other = around(mine, "core", CORE, 1)
    far_a = around(left[: ZL // 2], "x", X, 1)
    far_b = around(right[ZL // 2 :], "x", X, -1)
    left_other = around(left, "core", CORE, 1)
    right_other = around(right, "core", CORE, 1)
    far = jnp.concatenate([far_a, far_b], axis=0)
    far_other = around(far, "core", CORE, 1)

    state = attend(where, queries, docs, [mine, mine_other], (0,), None, False)
    state = attend(where, queries, docs, [left, left_other], (X - 1,), state, False)
    state = attend(where, queries, docs, [right, right_other], (1,), state, False)
    attended = attend(where, queries, docs, [far, far_other], (2,), state, True)
    pieces = ring_over_y(attended)
    y = lax.axis_index("y").astype(jnp.int32).reshape(1)
    terms = project(y, pieces, weight)
    came = lax.all_to_all(terms, TP, split_axis=0, concat_axis=0, tiled=True)
    return collect(came)


def solution(mesh):
    fine = Mesh(mesh.devices.reshape(ZL, X, CORE, ZH, Y), AXES)
    in_specs = (P(CTX, TP), P(CTX, None), P(CTX, None), P(CTX), P(TP, CTX))
    return jax.shard_map(
        compute, mesh=fine, in_specs=in_specs, out_specs=P(CTX + TP, None), check_vma=False
    )
```

```python
import functools
import math

import jax
import jax.numpy as jnp
from jax import lax
from jax.experimental import pallas as pl
from jax.experimental.pallas import tpu as pltpu
from jax.sharding import Mesh, PartitionSpec as P

HEADS = 64
KV_HEADS = 8
HD = 128
ZL, X, CORE, ZH, Y = 4, 4, 2, 2, 8
AXES = ("zl", "x", "core", "zh", "y")
CTX = ("zl", "x", "core")
TP = ("zh", "y")
PAD = 8
NEG = -1e30
SCALE2 = math.log2(math.e) / math.sqrt(HD)


def attend_kernel(sources, first, last, where_ref, q_ref, docs_ref, *refs):
    n = len(sources)
    pieces = refs[: 2 * n]
    refs = refs[2 * n :]
    if not first:
        m_in, acc_in = refs[:2]
        refs = refs[2:]
    if last:
        out_ref, m_ref, acc_ref = refs
    else:
        m_ref, acc_ref = refs
    rows = q_ref.shape[0]
    heads = q_ref.shape[1] // HD
    my_z, my_x, my_core = where_ref[0], where_ref[1], where_ref[2]
    my_block = my_z * X + my_x
    if first:
        m_ref[...] = jnp.full_like(m_ref, NEG)
        acc_ref[...] = jnp.zeros_like(acc_ref)
    else:
        m_ref[...] = m_in[...]
        acc_ref[...] = acc_in[...]
    q_docs = docs_ref[...]
    q_first, q_last = jnp.min(q_docs[:PAD]), jnp.max(q_docs[rows - PAD :])
    ones = jnp.ones((rows, HD), jnp.bfloat16)
    wide = rows // HD

    def extent(own, other, z):
        head, tail = [
            [ref[z, rows : rows + PAD, lanes].astype(jnp.float32) for ref in (own, other)]
            for lanes in (slice(0, HD), slice(rows - HD, rows))
        ]
        return jnp.min(jnp.minimum(*head)), jnp.max(jnp.maximum(*tail))

    extents = [
        [extent(pieces[2 * at], pieces[2 * at + 1], z) for z in range(ZL)] for at in range(n)
    ]
    for at, offset in enumerate(sources):
        own, other = pieces[2 * at], pieces[2 * at + 1]
        their_x = lax.rem(my_x + offset, X)
        firsts = [low for low, _ in extents[at]]
        lasts = [high for _, high in extents[at]]

        def pick(values, z):
            value = values[0]
            for index in range(1, ZL):
                value = jnp.where(z == index, values[index], value)
            return value

        def block(z, carry, own=own, other=other, their_x=their_x, firsts=firsts, lasts=lasts):
            their_block = z * X + their_x
            k_first, k_last = pick(firsts, z), pick(lasts, z)
            needed = (their_block <= my_block) & (k_last >= q_first)
            whole = needed & (their_block < my_block) & (k_first >= q_last)

            def update(masked):
                if masked:
                    docs_own = own[z, rows : rows + PAD, :].astype(jnp.float32)
                    docs_other = other[z, rows : rows + PAD, :].astype(jnp.float32)
                    row = lax.broadcasted_iota(jnp.int32, (rows, rows), 0)
                    lane = lax.broadcasted_iota(jnp.int32, (rows, rows), 1)
                    q_pos = my_block * (2 * rows) + my_core * rows + row
                    k_pos = their_block * (2 * rows) + lane
                    allowed = []
                    for side, docs in ((my_core, docs_own), (1 - my_core, docs_other)):
                        same = jnp.broadcast_to(docs[:1], (rows, rows)) == jnp.concatenate(
                            [q_docs] * wide, axis=1
                        )
                        allowed.append(same & (k_pos + side * rows <= q_pos))
                keys = [ref[z, :rows, :HD] for ref in (own, other)]
                values = [
                    jnp.concatenate([ref[z, :rows, HD:], ones], axis=1) for ref in (own, other)
                ]

                def score(h):
                    q = q_ref[:, h * HD : (h + 1) * HD]
                    scores = [
                        lax.dot_general(
                            q, k, (((1,), (1,)), ((), ())), preferred_element_type=jnp.float32
                        )
                        for k in keys
                    ]
                    if masked:
                        scores = [jnp.where(a, s, NEG) for a, s in zip(allowed, scores)]
                    return scores

                ahead = score(0)
                for h in range(heads):
                    these = slice(h * rows, (h + 1) * rows)
                    scores = ahead
                    if h + 1 < heads:
                        ahead = score(h + 1)
                    old = m_ref[these, :]
                    top = jnp.max(jnp.maximum(scores[0], scores[1]), axis=1, keepdims=True)
                    new = jnp.maximum(old, top)
                    broad = jnp.concatenate([new] * wide, axis=1)
                    total = None
                    for side in range(2):
                        weights = jnp.exp2((scores[side] - broad) * SCALE2)
                        if masked:
                            weights = jnp.where(allowed[side], weights, 0.0)
                        term = jnp.dot(
                            weights.astype(jnp.bfloat16),
                            values[side],
                            preferred_element_type=jnp.float32,
                        )
                        total = term if total is None else total + term
                    keep = jnp.exp2((old - new) * SCALE2)
                    m_ref[these, :] = new
                    acc_ref[these, :] = (
                        acc_ref[these, :] * jnp.concatenate([keep, keep], axis=1) + total
                    )

            @pl.when(whole)
            def _():
                update(False)

            @pl.when(needed & jnp.logical_not(whole))
            def _():
                update(True)

            return carry

        lax.fori_loop(0, ZL, block, 0)

    if last:
        for h in range(heads):
            these = slice(h * rows, (h + 1) * rows)
            out_ref[:, h * HD : (h + 1) * HD] = (
                acc_ref[these, :HD] / acc_ref[these, HD:]
            ).astype(jnp.bfloat16)


def attend(where, q, docs, pieces, sources, state, last):
    rows, width = q.shape
    heads = width // HD
    first = state is None
    states = (
        jax.ShapeDtypeStruct((heads * rows, HD), jnp.float32),
        jax.ShapeDtypeStruct((heads * rows, 2 * HD), jnp.float32),
    )
    vmem = pl.BlockSpec(memory_space=pltpu.VMEM)
    inputs = [q, docs, *pieces] + ([] if first else list(state))
    blocks = ZL * len(sources)
    return pl.pallas_call(
        functools.partial(attend_kernel, sources, first, last),
        out_shape=jax.ShapeDtypeStruct((rows, width), jnp.bfloat16) if last else states,
        in_specs=[pl.BlockSpec(memory_space=pltpu.SMEM)] + [vmem] * len(inputs),
        out_specs=vmem if last else (vmem, vmem),
        scratch_shapes=[pltpu.VMEM(s.shape, s.dtype) for s in states] if last else [],
        compiler_params=pltpu.CompilerParams(vmem_limit_bytes=40 << 20),
        cost_estimate=pl.CostEstimate(
            flops=blocks * heads * rows * 2 * rows * HD * 6,
            bytes_accessed=blocks * rows * HD * 8,
            transcendentals=blocks * heads * rows * 2 * rows,
        ),
    )(where, *inputs)


def around(value, axis, size, step):
    return lax.ppermute(value, axis, [(i, (i + step) % size) for i in range(size)])


def ring_over_y(attended):
    half = attended.shape[0] // 2
    pieces = [(0, attended)]
    left = right = attended
    for step in range(1, Y // 2):
        if step == Y // 2 - 1:
            far = (around(left[:half], "y", Y, 2), around(right[half:], "y", Y, -2))
        left = around(left, "y", Y, 1)
        right = around(right, "y", Y, -1)
        pieces += [(-step, left), (step, right)]
    return pieces + [(Y // 2, far)]


def project_kernel(offsets, y_ref, *refs):
    pieces, (weight_ref, out_ref, held_ref, acc_ref, sems) = refs[: Y + 1], refs[Y + 1 :]
    half = acc_ref.shape[1] // 2
    width = acc_ref.shape[2]
    part = out_ref.shape[1]

    def copy(at, z):
        their_y = lax.rem(y_ref[0] + (offsets[at] + Y), Y)
        return pltpu.make_async_copy(
            weight_ref.at[z, their_y], held_ref.at[at, z], sems.at[at, z]
        )

    for at in range(Y):
        for z in range(ZL):
            copy(at, z).start()
    for at in range(Y):
        for z in range(ZL):
            copy(at, z).wait()
            if at < Y - 1:
                term = jnp.dot(
                    pieces[at][...], held_ref[at, z], preferred_element_type=jnp.float32
                )
                acc_ref[z] = term if at == 0 else acc_ref[z] + term
                continue
            for side in range(2):
                rows = slice(side * half, (side + 1) * half)
                term = jnp.dot(
                    pieces[at + side][...], held_ref[at, z], preferred_element_type=jnp.float32
                )
                done = (acc_ref[z, rows] + term).astype(jnp.bfloat16)
                out_ref[
                    side * half // part : (side + 1) * half // part,
                    :,
                    z * width : (z + 1) * width,
                ] = done.reshape(half // part, part, width)


def project(y, pieces, weight):
    rows, depth = pieces[0][1].shape
    width = weight.shape[2]
    weight = weight.reshape(ZL, X * CORE, depth, width)
    offsets = tuple(offset for offset, _ in pieces)
    blocks = [block for _, block in pieces[:-1]] + list(pieces[-1][1])
    whole = pl.BlockSpec(memory_space=pltpu.VMEM)
    out = (ZH * Y, rows // (ZH * Y), ZL * width)
    return pl.pallas_call(
        functools.partial(project_kernel, offsets),
        out_shape=jax.ShapeDtypeStruct(out, jnp.bfloat16),
        in_specs=[pl.BlockSpec(memory_space=pltpu.SMEM)]
        + [whole] * len(blocks)
        + [pl.BlockSpec(memory_space=pltpu.HBM)],
        out_specs=whole,
        scratch_shapes=[
            pltpu.VMEM((Y, ZL, depth, width), jnp.bfloat16),
            pltpu.VMEM((ZL, rows, width), jnp.float32),
            pltpu.SemaphoreType.DMA((Y, ZL)),
        ],
        compiler_params=pltpu.CompilerParams(vmem_limit_bytes=51 << 20),
        cost_estimate=pl.CostEstimate(
            flops=2 * Y * rows * depth * ZL * width,
            bytes_accessed=2 * (Y * depth * ZL * width + Y * rows * depth),
            transcendentals=0,
        ),
    )(y, *blocks, weight)


def collect_kernel(came_ref, out_ref):
    width = came_ref.shape[2] // ZL
    for y in range(Y):
        for z in range(ZL):
            columns = slice(z * width, (z + 1) * width)
            both = came_ref[y, :, columns].astype(jnp.float32) + came_ref[
                Y + y, :, columns
            ].astype(jnp.float32)
            block = z * X * CORE + y
            out_ref[:, block * width : (block + 1) * width] = both.astype(jnp.bfloat16)


def collect(came):
    vmem = pl.BlockSpec(memory_space=pltpu.VMEM)
    return pl.pallas_call(
        collect_kernel,
        out_shape=jax.ShapeDtypeStruct((came.shape[1], Y * came.shape[2]), jnp.bfloat16),
        in_specs=[vmem],
        out_specs=vmem,
    )(came)


def compute(queries, key_rows, value_rows, documents, out_weight):
    rows = queries.shape[0]
    heads_here = queries.shape[1] // HD
    swap = [(a * Y + b, b * Y + a) for a in range(X * CORE) for b in range(Y)]
    swapped = lax.ppermute(out_weight, ("x", "core", "y"), swap)
    weight = lax.all_gather(swapped, CTX, axis=0)

    kv = lax.axis_index(TP) * heads_here // (HEADS // KV_HEADS)
    own_keys = lax.dynamic_slice_in_dim(key_rows, kv * HD, HD, 1)
    own_values = lax.dynamic_slice_in_dim(value_rows, kv * HD, HD, 1)
    doc_rows = jnp.broadcast_to(documents.astype(jnp.bfloat16)[None, :], (PAD, rows))
    packed = jnp.concatenate(
        [jnp.concatenate([own_keys, own_values], axis=1), doc_rows], axis=0
    )
    where = jnp.stack([lax.axis_index(a) for a in CTX]).astype(jnp.int32)
    docs = jnp.broadcast_to(documents.astype(jnp.float32)[:, None], (rows, HD))

    mine = lax.all_gather(packed, "zl", axis=0)
    left = around(mine, "x", X, 1)
    right = around(mine, "x", X, -1)
    mine_other = around(mine, "core", CORE, 1)
    far_a = around(left[: ZL // 2], "x", X, 1)
    far_b = around(right[ZL // 2 :], "x", X, -1)
    left_other = around(left, "core", CORE, 1)
    right_other = around(right, "core", CORE, 1)
    far = jnp.concatenate([far_a, far_b], axis=0)
    far_other = around(far, "core", CORE, 1)

    state = attend(where, queries, docs, [mine, mine_other], (0,), None, False)
    state = attend(where, queries, docs, [left, left_other], (X - 1,), state, False)
    state = attend(where, queries, docs, [right, right_other], (1,), state, False)
    attended = attend(where, queries, docs, [far, far_other], (2,), state, True)
    pieces = ring_over_y(attended)
    y = lax.axis_index("y").astype(jnp.int32).reshape(1)
    terms = project(y, pieces, weight)
    came = lax.all_to_all(terms, TP, split_axis=0, concat_axis=0, tiled=True)
    return collect(came)


def solution(mesh):
    fine = Mesh(mesh.devices.reshape(ZL, X, CORE, ZH, Y), AXES)
    in_specs = (P(CTX, TP), P(CTX, None), P(CTX, None), P(CTX), P(TP, CTX))
    return jax.shard_map(
        compute, mesh=fine, in_specs=in_specs, out_specs=P(CTX + TP, None), check_vma=False
    )
```

```python
import functools
import math

import jax
import jax.numpy as jnp
from jax import lax
from jax.experimental import pallas as pl
from jax.experimental.pallas import tpu as pltpu
from jax.sharding import Mesh, PartitionSpec as P

HEADS = 64
KV_HEADS = 8
HD = 128
ZL, X, CORE, ZH, Y = 4, 4, 2, 2, 8
AXES = ("zl", "x", "core", "zh", "y")
CTX = ("zl", "x", "core")
TP = ("zh", "y")
PAD = 8
NEG = -1e30
SCALE2 = math.log2(math.e) / math.sqrt(HD)


def attend_kernel(sources, first, last, where_ref, q_ref, docs_ref, *refs):
    n = len(sources)
    pieces = refs[: 2 * n]
    refs = refs[2 * n :]
    if not first:
        m_in, acc_in = refs[:2]
        refs = refs[2:]
    if last:
        out_ref, m_ref, acc_ref = refs
    else:
        m_ref, acc_ref = refs
    rows = q_ref.shape[0]
    heads = q_ref.shape[1] // HD
    my_z, my_x, my_core = where_ref[0], where_ref[1], where_ref[2]
    my_block = my_z * X + my_x
    if first:
        m_ref[...] = jnp.full_like(m_ref, NEG)
        acc_ref[...] = jnp.zeros_like(acc_ref)
    else:
        m_ref[...] = m_in[...]
        acc_ref[...] = acc_in[...]
    q_docs = docs_ref[...]
    q_first, q_last = jnp.min(q_docs[:PAD]), jnp.max(q_docs[rows - PAD :])
    ones = jnp.ones((rows, HD), jnp.bfloat16)
    wide = rows // HD

    def extent(own, other, z):
        head, tail = [
            [ref[z, rows : rows + PAD, lanes].astype(jnp.float32) for ref in (own, other)]
            for lanes in (slice(0, HD), slice(rows - HD, rows))
        ]
        return jnp.min(jnp.minimum(*head)), jnp.max(jnp.maximum(*tail))

    extents = [
        [extent(pieces[2 * at], pieces[2 * at + 1], z) for z in range(ZL)] for at in range(n)
    ]
    for at, offset in enumerate(sources):
        own, other = pieces[2 * at], pieces[2 * at + 1]
        their_x = lax.rem(my_x + (1 - 2 * lax.rem(my_x, 2)) * offset + X, X)
        firsts = [low for low, _ in extents[at]]
        lasts = [high for _, high in extents[at]]

        def pick(values, z):
            value = values[0]
            for index in range(1, ZL):
                value = jnp.where(z == index, values[index], value)
            return value

        def block(z, carry, own=own, other=other, their_x=their_x, firsts=firsts, lasts=lasts):
            their_block = z * X + their_x
            k_first, k_last = pick(firsts, z), pick(lasts, z)
            needed = (their_block <= my_block) & (k_last >= q_first)
            whole = needed & (their_block < my_block) & (k_first >= q_last)

            def update(masked):
                if masked:
                    docs_own = own[z, rows : rows + PAD, :].astype(jnp.float32)
                    docs_other = other[z, rows : rows + PAD, :].astype(jnp.float32)
                    row = lax.broadcasted_iota(jnp.int32, (rows, rows), 0)
                    lane = lax.broadcasted_iota(jnp.int32, (rows, rows), 1)
                    q_pos = my_block * (2 * rows) + my_core * rows + row
                    k_pos = their_block * (2 * rows) + lane
                    allowed = []
                    for side, docs in ((my_core, docs_own), (1 - my_core, docs_other)):
                        same = jnp.broadcast_to(docs[:1], (rows, rows)) == jnp.concatenate(
                            [q_docs] * wide, axis=1
                        )
                        allowed.append(same & (k_pos + side * rows <= q_pos))
                keys = [ref[z, :rows, :HD] for ref in (own, other)]
                values = [
                    jnp.concatenate([ref[z, :rows, HD:], ones], axis=1) for ref in (own, other)
                ]

                def score(h):
                    q = q_ref[:, h * HD : (h + 1) * HD]
                    scores = [
                        lax.dot_general(
                            q, k, (((1,), (1,)), ((), ())), preferred_element_type=jnp.float32
                        )
                        for k in keys
                    ]
                    if masked:
                        scores = [jnp.where(a, s, NEG) for a, s in zip(allowed, scores)]
                    return scores

                ahead = score(0)
                for h in range(heads):
                    these = slice(h * rows, (h + 1) * rows)
                    scores = ahead
                    if h + 1 < heads:
                        ahead = score(h + 1)
                    old = m_ref[these, :]
                    top = jnp.max(jnp.maximum(scores[0], scores[1]), axis=1, keepdims=True)
                    new = jnp.maximum(old, top)
                    broad = jnp.concatenate([new] * wide, axis=1)
                    total = None
                    for side in range(2):
                        weights = jnp.exp2((scores[side] - broad) * SCALE2)
                        if masked:
                            weights = jnp.where(allowed[side], weights, 0.0)
                        term = jnp.dot(
                            weights.astype(jnp.bfloat16),
                            values[side],
                            preferred_element_type=jnp.float32,
                        )
                        total = term if total is None else total + term
                    keep = jnp.exp2((old - new) * SCALE2)
                    m_ref[these, :] = new
                    acc_ref[these, :] = (
                        acc_ref[these, :] * jnp.concatenate([keep, keep], axis=1) + total
                    )

            @pl.when(whole)
            def _():
                update(False)

            @pl.when(needed & jnp.logical_not(whole))
            def _():
                update(True)

            return carry

        lax.fori_loop(0, ZL, block, 0)

    if last:
        for h in range(heads):
            these = slice(h * rows, (h + 1) * rows)
            out_ref[:, h * HD : (h + 1) * HD] = (
                acc_ref[these, :HD] / acc_ref[these, HD:]
            ).astype(jnp.bfloat16)


def attend(where, q, docs, pieces, sources, state, last):
    rows, width = q.shape
    heads = width // HD
    first = state is None
    states = (
        jax.ShapeDtypeStruct((heads * rows, HD), jnp.float32),
        jax.ShapeDtypeStruct((heads * rows, 2 * HD), jnp.float32),
    )
    vmem = pl.BlockSpec(memory_space=pltpu.VMEM)
    inputs = [q, docs, *pieces] + ([] if first else list(state))
    blocks = ZL * len(sources)
    return pl.pallas_call(
        functools.partial(attend_kernel, sources, first, last),
        out_shape=jax.ShapeDtypeStruct((rows, width), jnp.bfloat16) if last else states,
        in_specs=[pl.BlockSpec(memory_space=pltpu.SMEM)] + [vmem] * len(inputs),
        out_specs=vmem if last else (vmem, vmem),
        scratch_shapes=[pltpu.VMEM(s.shape, s.dtype) for s in states] if last else [],
        compiler_params=pltpu.CompilerParams(vmem_limit_bytes=40 << 20),
        cost_estimate=pl.CostEstimate(
            flops=blocks * heads * rows * 2 * rows * HD * 6,
            bytes_accessed=blocks * rows * HD * 8,
            transcendentals=blocks * heads * rows * 2 * rows,
        ),
    )(where, *inputs)


def around(value, axis, size, step):
    return lax.ppermute(value, axis, [(i, (i + step) % size) for i in range(size)])


def pairs(value, axis, size, second):
    step = -1 if second else 1
    moves = [(i, (i + (step if i % 2 == 0 else -step)) % size) for i in range(size)]
    return lax.ppermute(value, axis, moves)


def ring_over_y(attended):
    half = attended.shape[0] // 2
    pieces = [(0, attended)]
    one = two = attended
    for step in range(1, Y // 2):
        one, two = (pairs(two, "y", Y, False), pairs(one, "y", Y, True))
        pieces += [(step, one), (-step, two)]
    far = (pairs(two[:half], "y", Y, False), pairs(one[half:], "y", Y, True))
    return pieces + [(Y // 2, far)]


def project_kernel(offsets, y_ref, *refs):
    pieces, (weight_ref, out_ref, held_ref, acc_ref, sems) = refs[: Y + 1], refs[Y + 1 :]
    half = acc_ref.shape[1] // 2
    width = acc_ref.shape[2]
    part = out_ref.shape[1]

    def copy(at, z):
        sign = 1 - 2 * lax.rem(y_ref[0], 2)
        their_y = lax.rem(y_ref[0] + sign * offsets[at] + Y, Y)
        return pltpu.make_async_copy(
            weight_ref.at[z, their_y], held_ref.at[at, z], sems.at[at, z]
        )

    for at in range(Y):
        for z in range(ZL):
            copy(at, z).start()
    for at in range(Y):
        for z in range(ZL):
            copy(at, z).wait()
            if at < Y - 1:
                term = jnp.dot(
                    pieces[at][...], held_ref[at, z], preferred_element_type=jnp.float32
                )
                acc_ref[z] = term if at == 0 else acc_ref[z] + term
                continue
            for side in range(2):
                rows = slice(side * half, (side + 1) * half)
                term = jnp.dot(
                    pieces[at + side][...], held_ref[at, z], preferred_element_type=jnp.float32
                )
                done = (acc_ref[z, rows] + term).astype(jnp.bfloat16)
                out_ref[
                    side * half // part : (side + 1) * half // part,
                    :,
                    z * width : (z + 1) * width,
                ] = done.reshape(half // part, part, width)


def project(y, pieces, weight):
    rows, depth = pieces[0][1].shape
    width = weight.shape[2]
    weight = weight.reshape(ZL, X * CORE, depth, width)
    offsets = tuple(offset for offset, _ in pieces)
    blocks = [block for _, block in pieces[:-1]] + list(pieces[-1][1])
    whole = pl.BlockSpec(memory_space=pltpu.VMEM)
    out = (ZH * Y, rows // (ZH * Y), ZL * width)
    return pl.pallas_call(
        functools.partial(project_kernel, offsets),
        out_shape=jax.ShapeDtypeStruct(out, jnp.bfloat16),
        in_specs=[pl.BlockSpec(memory_space=pltpu.SMEM)]
        + [whole] * len(blocks)
        + [pl.BlockSpec(memory_space=pltpu.HBM)],
        out_specs=whole,
        scratch_shapes=[
            pltpu.VMEM((Y, ZL, depth, width), jnp.bfloat16),
            pltpu.VMEM((ZL, rows, width), jnp.float32),
            pltpu.SemaphoreType.DMA((Y, ZL)),
        ],
        compiler_params=pltpu.CompilerParams(vmem_limit_bytes=51 << 20),
        cost_estimate=pl.CostEstimate(
            flops=2 * Y * rows * depth * ZL * width,
            bytes_accessed=2 * (Y * depth * ZL * width + Y * rows * depth),
            transcendentals=0,
        ),
    )(y, *blocks, weight)


def collect_kernel(came_ref, out_ref):
    width = came_ref.shape[2] // ZL
    for y in range(Y):
        for z in range(ZL):
            columns = slice(z * width, (z + 1) * width)
            both = came_ref[y, :, columns].astype(jnp.float32) + came_ref[
                Y + y, :, columns
            ].astype(jnp.float32)
            block = z * X * CORE + y
            out_ref[:, block * width : (block + 1) * width] = both.astype(jnp.bfloat16)


def collect(came):
    vmem = pl.BlockSpec(memory_space=pltpu.VMEM)
    return pl.pallas_call(
        collect_kernel,
        out_shape=jax.ShapeDtypeStruct((came.shape[1], Y * came.shape[2]), jnp.bfloat16),
        in_specs=[vmem],
        out_specs=vmem,
    )(came)


def compute(queries, key_rows, value_rows, documents, out_weight):
    rows = queries.shape[0]
    heads_here = queries.shape[1] // HD
    swap = [(a * Y + b, b * Y + a) for a in range(X * CORE) for b in range(Y)]
    swapped = lax.ppermute(out_weight, ("x", "core", "y"), swap)
    weight = lax.all_gather(swapped, CTX, axis=0)

    kv = lax.axis_index(TP) * heads_here // (HEADS // KV_HEADS)
    own_keys = lax.dynamic_slice_in_dim(key_rows, kv * HD, HD, 1)
    own_values = lax.dynamic_slice_in_dim(value_rows, kv * HD, HD, 1)
    doc_rows = jnp.broadcast_to(documents.astype(jnp.bfloat16)[None, :], (PAD, rows))
    packed = jnp.concatenate(
        [jnp.concatenate([own_keys, own_values], axis=1), doc_rows], axis=0
    )
    where = jnp.stack([lax.axis_index(a) for a in CTX]).astype(jnp.int32)
    docs = jnp.broadcast_to(documents.astype(jnp.float32)[:, None], (rows, HD))

    mine = lax.all_gather(packed, "zl", axis=0)
    one = pairs(mine, "x", X, False)
    two = pairs(mine, "x", X, True)
    mine_other = around(mine, "core", CORE, 1)
    far_two = pairs(one[ZL // 2 :], "x", X, True)
    one_other = around(one, "core", CORE, 1)
    far_one = pairs(two[: ZL // 2], "x", X, False)
    two_other = around(two, "core", CORE, 1)
    far = jnp.concatenate([far_one, far_two], axis=0)
    far_other = around(far, "core", CORE, 1)

    state = attend(where, queries, docs, [mine, mine_other], (0,), None, False)
    state = attend(where, queries, docs, [one, one_other], (1,), state, False)
    state = attend(where, queries, docs, [two, two_other], (-1,), state, False)
    attended = attend(where, queries, docs, [far, far_other], (2,), state, True)
    pieces = ring_over_y(attended)
    y = lax.axis_index("y").astype(jnp.int32).reshape(1)
    terms = project(y, pieces, weight)
    came = lax.all_to_all(terms, TP, split_axis=0, concat_axis=0, tiled=True)
    return collect(came)


def solution(mesh):
    fine = Mesh(mesh.devices.reshape(ZL, X, CORE, ZH, Y), AXES)
    in_specs = (P(CTX, TP), P(CTX, None), P(CTX, None), P(CTX), P(TP, CTX))
    return jax.shard_map(
        compute, mesh=fine, in_specs=in_specs, out_specs=P(CTX + TP, None), check_vma=False
    )
```

```python
import functools
import math

import jax
import jax.numpy as jnp
from jax import lax
from jax.experimental import pallas as pl
from jax.experimental.pallas import tpu as pltpu
from jax.sharding import Mesh, PartitionSpec as P

HEADS = 64
KV_HEADS = 8
HD = 128
ZL, X, CORE, ZH, Y = 4, 4, 2, 2, 8
AXES = ("zl", "x", "core", "zh", "y")
CTX = ("zl", "x", "core")
TP = ("zh", "y")
PAD = 8
EARLY = 7
NEG = -1e30
SCALE2 = math.log2(math.e) / math.sqrt(HD)


def attend_kernel(sources, first, last, where_ref, q_ref, docs_ref, *refs):
    n = len(sources)
    pieces = refs[: 2 * n]
    refs = refs[2 * n :]
    if not first:
        m_in, acc_in = refs[:2]
        refs = refs[2:]
    if last:
        out_ref, m_ref, acc_ref = refs
    else:
        m_ref, acc_ref = refs
    rows = q_ref.shape[0]
    heads = q_ref.shape[1] // HD
    my_z, my_x, my_core = where_ref[0], where_ref[1], where_ref[2]
    my_block = my_z * X + my_x
    if first:
        m_ref[...] = jnp.full_like(m_ref, NEG)
        acc_ref[...] = jnp.zeros_like(acc_ref)
    else:
        m_ref[...] = m_in[...]
        acc_ref[...] = acc_in[...]
    q_docs = docs_ref[...]
    q_first, q_last = jnp.min(q_docs[:PAD]), jnp.max(q_docs[rows - PAD :])
    ones = jnp.ones((rows, HD), jnp.bfloat16)
    wide = rows // HD

    def extent(own, other, z):
        head, tail = [
            [ref[z, rows : rows + PAD, lanes].astype(jnp.float32) for ref in (own, other)]
            for lanes in (slice(0, HD), slice(rows - HD, rows))
        ]
        return jnp.min(jnp.minimum(*head)), jnp.max(jnp.maximum(*tail))

    extents = [
        [extent(pieces[2 * at], pieces[2 * at + 1], z) for z in range(ZL)] for at in range(n)
    ]
    for at, offset in enumerate(sources):
        own, other = pieces[2 * at], pieces[2 * at + 1]
        their_x = lax.rem(my_x + (1 - 2 * lax.rem(my_x, 2)) * offset + X, X)
        firsts = [low for low, _ in extents[at]]
        lasts = [high for _, high in extents[at]]

        def pick(values, z):
            value = values[0]
            for index in range(1, ZL):
                value = jnp.where(z == index, values[index], value)
            return value

        def block(z, carry, own=own, other=other, their_x=their_x, firsts=firsts, lasts=lasts):
            their_block = z * X + their_x
            k_first, k_last = pick(firsts, z), pick(lasts, z)
            needed = (their_block <= my_block) & (k_last >= q_first)
            whole = needed & (their_block < my_block) & (k_first >= q_last)

            def update(masked):
                if masked:
                    docs_own = own[z, rows : rows + PAD, :].astype(jnp.float32)
                    docs_other = other[z, rows : rows + PAD, :].astype(jnp.float32)
                    row = lax.broadcasted_iota(jnp.int32, (rows, rows), 0)
                    lane = lax.broadcasted_iota(jnp.int32, (rows, rows), 1)
                    q_pos = my_block * (2 * rows) + my_core * rows + row
                    k_pos = their_block * (2 * rows) + lane
                    allowed = []
                    for side, docs in ((my_core, docs_own), (1 - my_core, docs_other)):
                        same = jnp.broadcast_to(docs[:1], (rows, rows)) == jnp.concatenate(
                            [q_docs] * wide, axis=1
                        )
                        allowed.append(same & (k_pos + side * rows <= q_pos))
                keys = [ref[z, :rows, :HD] for ref in (own, other)]
                values = [
                    jnp.concatenate([ref[z, :rows, HD:], ones], axis=1) for ref in (own, other)
                ]

                def score(h):
                    q = q_ref[:, h * HD : (h + 1) * HD]
                    scores = [
                        lax.dot_general(
                            q, k, (((1,), (1,)), ((), ())), preferred_element_type=jnp.float32
                        )
                        for k in keys
                    ]
                    if masked:
                        scores = [jnp.where(a, s, NEG) for a, s in zip(allowed, scores)]
                    return scores

                ahead = score(0)
                for h in range(heads):
                    these = slice(h * rows, (h + 1) * rows)
                    scores = ahead
                    if h + 1 < heads:
                        ahead = score(h + 1)
                    old = m_ref[these, :]
                    top = jnp.max(jnp.maximum(scores[0], scores[1]), axis=1, keepdims=True)
                    new = jnp.maximum(old, top)
                    broad = jnp.concatenate([new] * wide, axis=1)
                    total = None
                    for side in range(2):
                        weights = jnp.exp2((scores[side] - broad) * SCALE2)
                        if masked:
                            weights = jnp.where(allowed[side], weights, 0.0)
                        term = jnp.dot(
                            weights.astype(jnp.bfloat16),
                            values[side],
                            preferred_element_type=jnp.float32,
                        )
                        total = term if total is None else total + term
                    keep = jnp.exp2((old - new) * SCALE2)
                    m_ref[these, :] = new
                    acc_ref[these, :] = (
                        acc_ref[these, :] * jnp.concatenate([keep, keep], axis=1) + total
                    )

            @pl.when(whole)
            def _():
                update(False)

            @pl.when(needed & jnp.logical_not(whole))
            def _():
                update(True)

            return carry

        lax.fori_loop(0, ZL, block, 0)

    if last:
        for h in range(heads):
            these = slice(h * rows, (h + 1) * rows)
            out_ref[:, h * HD : (h + 1) * HD] = (
                acc_ref[these, :HD] / acc_ref[these, HD:]
            ).astype(jnp.bfloat16)


def attend(where, q, docs, pieces, sources, state, last):
    rows, width = q.shape
    heads = width // HD
    first = state is None
    states = (
        jax.ShapeDtypeStruct((heads * rows, HD), jnp.float32),
        jax.ShapeDtypeStruct((heads * rows, 2 * HD), jnp.float32),
    )
    vmem = pl.BlockSpec(memory_space=pltpu.VMEM)
    inputs = [q, docs, *pieces] + ([] if first else list(state))
    blocks = ZL * len(sources)
    return pl.pallas_call(
        functools.partial(attend_kernel, sources, first, last),
        out_shape=jax.ShapeDtypeStruct((rows, width), jnp.bfloat16) if last else states,
        in_specs=[pl.BlockSpec(memory_space=pltpu.SMEM)] + [vmem] * len(inputs),
        out_specs=vmem if last else (vmem, vmem),
        scratch_shapes=[pltpu.VMEM(s.shape, s.dtype) for s in states] if last else [],
        compiler_params=pltpu.CompilerParams(vmem_limit_bytes=40 << 20),
        cost_estimate=pl.CostEstimate(
            flops=blocks * heads * rows * 2 * rows * HD * 6,
            bytes_accessed=blocks * rows * HD * 8,
            transcendentals=blocks * heads * rows * 2 * rows,
        ),
    )(where, *inputs)


def around(value, axis, size, step):
    return lax.ppermute(value, axis, [(i, (i + step) % size) for i in range(size)])


def pairs(value, axis, size, second):
    step = -1 if second else 1
    moves = [(i, (i + (step if i % 2 == 0 else -step)) % size) for i in range(size)]
    return lax.ppermute(value, axis, moves)


def ring_over_y(attended):
    half = attended.shape[0] // 2
    pieces = [(0, attended)]
    one = two = attended
    for step in range(1, Y // 2):
        one, two = (pairs(two, "y", Y, False), pairs(one, "y", Y, True))
        pieces += [(step, one), (-step, two)]
    far = (pairs(two[:half], "y", Y, False), pairs(one[half:], "y", Y, True))
    return pieces + [(Y // 2, far)]


def project_kernel(offsets, first, y_ref, *refs):
    count = len(offsets)
    if first:
        blocks, (weight_ref, acc_ref, held_ref, sems) = refs[:count], refs[count:]
    else:
        blocks, (weight_ref, acc_ref, out_ref, held_ref, sems) = refs[: count + 1], refs[count + 1 :]
    half = acc_ref.shape[1] // 2
    width = acc_ref.shape[2]
    sign = 1 - 2 * lax.rem(y_ref[0], 2)

    def copy(at, z):
        their_y = lax.rem(y_ref[0] + sign * offsets[at] + Y, Y)
        return pltpu.make_async_copy(
            weight_ref.at[z, their_y], held_ref.at[at, z], sems.at[at, z]
        )

    def term(block, at, z):
        return jnp.dot(block, held_ref[at, z], preferred_element_type=jnp.float32)

    for at in range(count):
        for z in range(ZL):
            copy(at, z).start()
    if first:
        for at in range(count):
            for z in range(ZL):
                copy(at, z).wait()
                new = term(blocks[at][...], at, z)
                acc_ref[z] = new if at == 0 else acc_ref[z] + new
        return
    part = out_ref.shape[1]
    for at in range(count):
        for z in range(ZL):
            copy(at, z).wait()
    for z in range(ZL):
        for side in range(2):
            rows = slice(side * half, (side + 1) * half)
            total = acc_ref[z, rows]
            for at in range(count - 1):
                total = total + term(blocks[at][rows, :], at, z)
            total = total + term(blocks[count - 1 + side][...], count - 1, z)
            out_ref[
                side * half // part : (side + 1) * half // part, :, z * width : (z + 1) * width
            ] = total.astype(jnp.bfloat16).reshape(half // part, part, width)


def project(y, pieces, weight, total):
    first = total is None
    rows = pieces[0][1].shape[0] if first else total.shape[1]
    depth, width = weight.shape[1:]
    count = len(pieces)
    weight = weight.reshape(ZL, X * CORE, depth, width)
    offsets = tuple(offset for offset, _ in pieces)
    blocks = [block for _, block in pieces]
    if not first:
        blocks = blocks[:-1] + list(blocks[-1])
    whole = pl.BlockSpec(memory_space=pltpu.VMEM)
    sums = jax.ShapeDtypeStruct((ZL, rows, width), jnp.float32)
    out = jax.ShapeDtypeStruct((ZH * Y, rows // (ZH * Y), ZL * width), jnp.bfloat16)
    return pl.pallas_call(
        functools.partial(project_kernel, offsets, first),
        out_shape=sums if first else out,
        in_specs=[pl.BlockSpec(memory_space=pltpu.SMEM)]
        + [whole] * len(blocks)
        + [pl.BlockSpec(memory_space=pltpu.HBM)]
        + [whole] * (0 if first else 1),
        out_specs=whole,
        scratch_shapes=[
            pltpu.VMEM((count, ZL, depth, width), jnp.bfloat16),
            pltpu.SemaphoreType.DMA((count, ZL)),
        ],
        compiler_params=pltpu.CompilerParams(vmem_limit_bytes=51 << 20),
        cost_estimate=pl.CostEstimate(
            flops=2 * count * rows * depth * ZL * width,
            bytes_accessed=2 * (count * depth * ZL * width + count * rows * depth),
            transcendentals=0,
        ),
    )(y, *blocks, weight, *(() if first else (total,)))


def collect_kernel(came_ref, out_ref):
    width = came_ref.shape[2] // ZL
    for y in range(Y):
        for z in range(ZL):
            columns = slice(z * width, (z + 1) * width)
            both = came_ref[y, :, columns].astype(jnp.float32) + came_ref[
                Y + y, :, columns
            ].astype(jnp.float32)
            block = z * X * CORE + y
            out_ref[:, block * width : (block + 1) * width] = both.astype(jnp.bfloat16)


def collect(came):
    vmem = pl.BlockSpec(memory_space=pltpu.VMEM)
    return pl.pallas_call(
        collect_kernel,
        out_shape=jax.ShapeDtypeStruct((came.shape[1], Y * came.shape[2]), jnp.bfloat16),
        in_specs=[vmem],
        out_specs=vmem,
    )(came)


def compute(queries, key_rows, value_rows, documents, out_weight):
    rows = queries.shape[0]
    heads_here = queries.shape[1] // HD
    swap = [(a * Y + b, b * Y + a) for a in range(X * CORE) for b in range(Y)]
    swapped = lax.ppermute(out_weight, ("x", "core", "y"), swap)
    weight = lax.all_gather(swapped, CTX, axis=0)

    kv = lax.axis_index(TP) * heads_here // (HEADS // KV_HEADS)
    own_keys = lax.dynamic_slice_in_dim(key_rows, kv * HD, HD, 1)
    own_values = lax.dynamic_slice_in_dim(value_rows, kv * HD, HD, 1)
    doc_rows = jnp.broadcast_to(documents.astype(jnp.bfloat16)[None, :], (PAD, rows))
    packed = jnp.concatenate(
        [jnp.concatenate([own_keys, own_values], axis=1), doc_rows], axis=0
    )
    where = jnp.stack([lax.axis_index(a) for a in CTX]).astype(jnp.int32)
    docs = jnp.broadcast_to(documents.astype(jnp.float32)[:, None], (rows, HD))

    mine = lax.all_gather(packed, "zl", axis=0)
    one = pairs(mine, "x", X, False)
    two = pairs(mine, "x", X, True)
    mine_other = around(mine, "core", CORE, 1)
    far_two = pairs(one[ZL // 2 :], "x", X, True)
    one_other = around(one, "core", CORE, 1)
    far_one = pairs(two[: ZL // 2], "x", X, False)
    two_other = around(two, "core", CORE, 1)
    far = jnp.concatenate([far_one, far_two], axis=0)
    far_other = around(far, "core", CORE, 1)

    state = attend(where, queries, docs, [mine, mine_other], (0,), None, False)
    state = attend(where, queries, docs, [one, one_other], (1,), state, False)
    state = attend(where, queries, docs, [two, two_other], (-1,), state, False)
    attended = attend(where, queries, docs, [far, far_other], (2,), state, True)
    pieces = ring_over_y(attended)
    y = lax.axis_index("y").astype(jnp.int32).reshape(1)
    total = project(y, pieces[:EARLY], weight, None)
    terms = project(y, pieces[EARLY:], weight, total)
    came = lax.all_to_all(terms, TP, split_axis=0, concat_axis=0, tiled=True)
    return collect(came)


def solution(mesh):
    fine = Mesh(mesh.devices.reshape(ZL, X, CORE, ZH, Y), AXES)
    in_specs = (P(CTX, TP), P(CTX, None), P(CTX, None), P(CTX), P(TP, CTX))
    return jax.shard_map(
        compute, mesh=fine, in_specs=in_specs, out_specs=P(CTX + TP, None), check_vma=False
    )
```

```python
import functools
import math

import jax
import jax.numpy as jnp
from jax import lax
from jax.experimental import pallas as pl
from jax.experimental.pallas import tpu as pltpu
from jax.sharding import Mesh, PartitionSpec as P

HEADS = 64
KV_HEADS = 8
HD = 128
ZL, X, CORE, ZH, Y = 4, 4, 2, 2, 8
AXES = ("zl", "x", "core", "zh", "y")
CTX = ("zl", "x", "core")
TP = ("zh", "y")
PAD = 8
EARLY = 7
NEG = -1e30
SCALE2 = math.log2(math.e) / math.sqrt(HD)


def attend_kernel(sources, first, last, where_ref, q_ref, docs_ref, *refs):
    n = len(sources)
    pieces = refs[: 2 * n]
    refs = refs[2 * n :]
    if not first:
        m_in, acc_in = refs[:2]
        refs = refs[2:]
    if last:
        out_ref, m_ref, acc_ref = refs
    else:
        m_ref, acc_ref = refs
    rows = q_ref.shape[0]
    heads = q_ref.shape[1] // HD
    my_z, my_x, my_core = where_ref[0], where_ref[1], where_ref[2]
    my_block = my_z * X + my_x
    if first:
        m_ref[...] = jnp.full_like(m_ref, NEG)
        acc_ref[...] = jnp.zeros_like(acc_ref)
    else:
        m_ref[...] = m_in[...]
        acc_ref[...] = acc_in[...]
    q_docs = docs_ref[...]
    q_first, q_last = jnp.min(q_docs[:PAD]), jnp.max(q_docs[rows - PAD :])
    ones = jnp.ones((rows, HD), jnp.bfloat16)
    wide = rows // HD

    def extent(own, other, z):
        head, tail = [
            [ref[z, rows : rows + PAD, lanes].astype(jnp.float32) for ref in (own, other)]
            for lanes in (slice(0, HD), slice(rows - HD, rows))
        ]
        return jnp.min(jnp.minimum(*head)), jnp.max(jnp.maximum(*tail))

    extents = [
        [extent(pieces[2 * at], pieces[2 * at + 1], z) for z in range(ZL)] for at in range(n)
    ]
    for at, offset in enumerate(sources):
        own, other = pieces[2 * at], pieces[2 * at + 1]
        their_x = lax.rem(my_x + offset, X)
        firsts = [low for low, _ in extents[at]]
        lasts = [high for _, high in extents[at]]

        def pick(values, z):
            value = values[0]
            for index in range(1, ZL):
                value = jnp.where(z == index, values[index], value)
            return value

        def block(z, carry, own=own, other=other, their_x=their_x, firsts=firsts, lasts=lasts):
            their_block = z * X + their_x
            k_first, k_last = pick(firsts, z), pick(lasts, z)
            needed = (their_block <= my_block) & (k_last >= q_first)
            whole = needed & (their_block < my_block) & (k_first >= q_last)

            def update(masked):
                if masked:
                    docs_own = own[z, rows : rows + PAD, :].astype(jnp.float32)
                    docs_other = other[z, rows : rows + PAD, :].astype(jnp.float32)
                    row = lax.broadcasted_iota(jnp.int32, (rows, rows), 0)
                    lane = lax.broadcasted_iota(jnp.int32, (rows, rows), 1)
                    q_pos = my_block * (2 * rows) + my_core * rows + row
                    k_pos = their_block * (2 * rows) + lane
                    allowed = []
                    for side, docs in ((my_core, docs_own), (1 - my_core, docs_other)):
                        same = jnp.broadcast_to(docs[:1], (rows, rows)) == jnp.concatenate(
                            [q_docs] * wide, axis=1
                        )
                        allowed.append(same & (k_pos + side * rows <= q_pos))
                keys = [ref[z, :rows, :HD] for ref in (own, other)]
                values = [
                    jnp.concatenate([ref[z, :rows, HD:], ones], axis=1) for ref in (own, other)
                ]

                def score(h):
                    q = q_ref[:, h * HD : (h + 1) * HD]
                    scores = [
                        lax.dot_general(
                            q, k, (((1,), (1,)), ((), ())), preferred_element_type=jnp.float32
                        )
                        for k in keys
                    ]
                    if masked:
                        scores = [jnp.where(a, s, NEG) for a, s in zip(allowed, scores)]
                    return scores

                ahead = score(0)
                for h in range(heads):
                    these = slice(h * rows, (h + 1) * rows)
                    scores = ahead
                    if h + 1 < heads:
                        ahead = score(h + 1)
                    old = m_ref[these, :]
                    top = jnp.max(jnp.maximum(scores[0], scores[1]), axis=1, keepdims=True)
                    new = jnp.maximum(old, top)
                    broad = jnp.concatenate([new] * wide, axis=1)
                    total = None
                    for side in range(2):
                        weights = jnp.exp2((scores[side] - broad) * SCALE2)
                        if masked:
                            weights = jnp.where(allowed[side], weights, 0.0)
                        term = jnp.dot(
                            weights.astype(jnp.bfloat16),
                            values[side],
                            preferred_element_type=jnp.float32,
                        )
                        total = term if total is None else total + term
                    keep = jnp.exp2((old - new) * SCALE2)
                    m_ref[these, :] = new
                    acc_ref[these, :] = (
                        acc_ref[these, :] * jnp.concatenate([keep, keep], axis=1) + total
                    )

            @pl.when(whole)
            def _():
                update(False)

            @pl.when(needed & jnp.logical_not(whole))
            def _():
                update(True)

            return carry

        lax.fori_loop(0, ZL, block, 0)

    if last:
        for h in range(heads):
            these = slice(h * rows, (h + 1) * rows)
            out_ref[:, h * HD : (h + 1) * HD] = (
                acc_ref[these, :HD] / acc_ref[these, HD:]
            ).astype(jnp.bfloat16)


def attend(where, q, docs, pieces, sources, state, last):
    rows, width = q.shape
    heads = width // HD
    first = state is None
    states = (
        jax.ShapeDtypeStruct((heads * rows, HD), jnp.float32),
        jax.ShapeDtypeStruct((heads * rows, 2 * HD), jnp.float32),
    )
    vmem = pl.BlockSpec(memory_space=pltpu.VMEM)
    inputs = [q, docs, *pieces] + ([] if first else list(state))
    blocks = ZL * len(sources)
    return pl.pallas_call(
        functools.partial(attend_kernel, sources, first, last),
        out_shape=jax.ShapeDtypeStruct((rows, width), jnp.bfloat16) if last else states,
        in_specs=[pl.BlockSpec(memory_space=pltpu.SMEM)] + [vmem] * len(inputs),
        out_specs=vmem if last else (vmem, vmem),
        scratch_shapes=[pltpu.VMEM(s.shape, s.dtype) for s in states] if last else [],
        compiler_params=pltpu.CompilerParams(vmem_limit_bytes=40 << 20),
        cost_estimate=pl.CostEstimate(
            flops=blocks * heads * rows * 2 * rows * HD * 6,
            bytes_accessed=blocks * rows * HD * 8,
            transcendentals=blocks * heads * rows * 2 * rows,
        ),
    )(where, *inputs)


def around(value, axis, size, step):
    return lax.ppermute(value, axis, [(i, (i + step) % size) for i in range(size)])


def pairs(value, axis, size, second):
    step = -1 if second else 1
    moves = [(i, (i + (step if i % 2 == 0 else -step)) % size) for i in range(size)]
    return lax.ppermute(value, axis, moves)


def ring_over_y(attended):
    half = attended.shape[0] // 2
    pieces = [(0, attended)]
    one = two = attended
    for step in range(1, Y // 2):
        one, two = (pairs(two, "y", Y, False), pairs(one, "y", Y, True))
        pieces += [(step, one), (-step, two)]
    far = (pairs(two[:half], "y", Y, False), pairs(one[half:], "y", Y, True))
    return pieces + [(Y // 2, far)]


def project_kernel(offsets, first, y_ref, *refs):
    count = len(offsets)
    if first:
        blocks, (weight_ref, acc_ref, held_ref, sems) = refs[:count], refs[count:]
    else:
        blocks, (weight_ref, acc_ref, out_ref, held_ref, sems) = refs[: count + 1], refs[count + 1 :]
    half = acc_ref.shape[1] // 2
    width = acc_ref.shape[2]
    sign = 1 - 2 * lax.rem(y_ref[0], 2)

    def copy(at, z):
        their_y = lax.rem(y_ref[0] + sign * offsets[at] + Y, Y)
        return pltpu.make_async_copy(
            weight_ref.at[z, their_y], held_ref.at[at, z], sems.at[at, z]
        )

    def term(block, at, z):
        return jnp.dot(block, held_ref[at, z], preferred_element_type=jnp.float32)

    for at in range(count):
        for z in range(ZL):
            copy(at, z).start()
    if first:
        for at in range(count):
            for z in range(ZL):
                copy(at, z).wait()
                new = term(blocks[at][...], at, z)
                acc_ref[z] = new if at == 0 else acc_ref[z] + new
        return
    part = out_ref.shape[1]
    for at in range(count):
        for z in range(ZL):
            copy(at, z).wait()
    for z in range(ZL):
        for side in range(2):
            rows = slice(side * half, (side + 1) * half)
            total = acc_ref[z, rows]
            for at in range(count - 1):
                total = total + term(blocks[at][rows, :], at, z)
            total = total + term(blocks[count - 1 + side][...], count - 1, z)
            out_ref[
                side * half // part : (side + 1) * half // part, :, z * width : (z + 1) * width
            ] = total.astype(jnp.bfloat16).reshape(half // part, part, width)


def project(y, pieces, weight, total):
    first = total is None
    rows = pieces[0][1].shape[0] if first else total.shape[1]
    depth, width = weight.shape[1:]
    count = len(pieces)
    weight = weight.reshape(ZL, X * CORE, depth, width)
    offsets = tuple(offset for offset, _ in pieces)
    blocks = [block for _, block in pieces]
    if not first:
        blocks = blocks[:-1] + list(blocks[-1])
    whole = pl.BlockSpec(memory_space=pltpu.VMEM)
    sums = jax.ShapeDtypeStruct((ZL, rows, width), jnp.float32)
    out = jax.ShapeDtypeStruct((ZH * Y, rows // (ZH * Y), ZL * width), jnp.bfloat16)
    return pl.pallas_call(
        functools.partial(project_kernel, offsets, first),
        out_shape=sums if first else out,
        in_specs=[pl.BlockSpec(memory_space=pltpu.SMEM)]
        + [whole] * len(blocks)
        + [pl.BlockSpec(memory_space=pltpu.HBM)]
        + [whole] * (0 if first else 1),
        out_specs=whole,
        scratch_shapes=[
            pltpu.VMEM((count, ZL, depth, width), jnp.bfloat16),
            pltpu.SemaphoreType.DMA((count, ZL)),
        ],
        compiler_params=pltpu.CompilerParams(vmem_limit_bytes=51 << 20),
        cost_estimate=pl.CostEstimate(
            flops=2 * count * rows * depth * ZL * width,
            bytes_accessed=2 * (count * depth * ZL * width + count * rows * depth),
            transcendentals=0,
        ),
    )(y, *blocks, weight, *(() if first else (total,)))


def collect_kernel(came_ref, out_ref):
    width = came_ref.shape[2] // ZL
    for y in range(Y):
        for z in range(ZL):
            columns = slice(z * width, (z + 1) * width)
            both = came_ref[y, :, columns].astype(jnp.float32) + came_ref[
                Y + y, :, columns
            ].astype(jnp.float32)
            block = z * X * CORE + y
            out_ref[:, block * width : (block + 1) * width] = both.astype(jnp.bfloat16)


def collect(came):
    vmem = pl.BlockSpec(memory_space=pltpu.VMEM)
    return pl.pallas_call(
        collect_kernel,
        out_shape=jax.ShapeDtypeStruct((came.shape[1], Y * came.shape[2]), jnp.bfloat16),
        in_specs=[vmem],
        out_specs=vmem,
    )(came)


def compute(queries, key_rows, value_rows, documents, out_weight):
    rows = queries.shape[0]
    heads_here = queries.shape[1] // HD
    swap = [(a * Y + b, b * Y + a) for a in range(X * CORE) for b in range(Y)]
    swapped = lax.ppermute(out_weight, ("x", "core", "y"), swap)
    weight = lax.all_gather(swapped, CTX, axis=0)

    kv = lax.axis_index(TP) * heads_here // (HEADS // KV_HEADS)
    own_keys = lax.dynamic_slice_in_dim(key_rows, kv * HD, HD, 1)
    own_values = lax.dynamic_slice_in_dim(value_rows, kv * HD, HD, 1)
    doc_rows = jnp.broadcast_to(documents.astype(jnp.bfloat16)[None, :], (PAD, rows))
    packed = jnp.concatenate(
        [jnp.concatenate([own_keys, own_values], axis=1), doc_rows], axis=0
    )
    where = jnp.stack([lax.axis_index(a) for a in CTX]).astype(jnp.int32)
    docs = jnp.broadcast_to(documents.astype(jnp.float32)[:, None], (rows, HD))

    mine = lax.all_gather(packed, "zl", axis=0)
    left = around(mine, "x", X, 1)
    right = around(mine, "x", X, -1)
    mine_other = around(mine, "core", CORE, 1)
    far_a = around(left[: ZL // 2], "x", X, 1)
    left_other = around(left, "core", CORE, 1)
    far_b = around(right[ZL // 2 :], "x", X, -1)
    right_other = around(right, "core", CORE, 1)
    far = jnp.concatenate([far_a, far_b], axis=0)
    far_other = around(far, "core", CORE, 1)

    state = attend(where, queries, docs, [mine, mine_other], (0,), None, False)
    sides = [left, left_other, right, right_other]
    state = attend(where, queries, docs, sides, (X - 1, 1), state, False)
    attended = attend(where, queries, docs, [far, far_other], (2,), state, True)
    pieces = ring_over_y(attended)
    y = lax.axis_index("y").astype(jnp.int32).reshape(1)
    total = project(y, pieces[:EARLY], weight, None)
    terms = project(y, pieces[EARLY:], weight, total)
    came = lax.all_to_all(terms, TP, split_axis=0, concat_axis=0, tiled=True)
    return collect(came)


def solution(mesh):
    fine = Mesh(mesh.devices.reshape(ZL, X, CORE, ZH, Y), AXES)
    in_specs = (P(CTX, TP), P(CTX, None), P(CTX, None), P(CTX), P(TP, CTX))
    return jax.shard_map(
        compute, mesh=fine, in_specs=in_specs, out_specs=P(CTX + TP, None), check_vma=False
    )
```
